32 devices in a mesh: space: 4 (over x, core), tm: 8 (over z, y).
Axes of the slice: x: 2, y: 2, z: 4, core: 2. Of those that a mesh axis runs over, the one named last changes fastest.
Arguments:
- snapshots: bfloat16 [4096, 65536], P('tm', 'space'), may hold values from -24 to 24
- freq_bins: int32 [2], replicated, may hold values from 1 to 127
Outputs:
- gram_matrix: float32 [2, 64, 64], replicated
- whitened: float32 [2, 64, 65536], P(None, None, ('space', 'tm'))
The draws below stay inside these ranges and needn't reach their ends.
All inputs are finite; a program needn't handle non-finite values.
Results may differ from the reference program's by a relative error of at most 0.0041.
Values may be sent and summed in bfloat16 or wider, within the bound.
No kernel may reach another device: no remote copies, remote signals or barrier semaphores. Data moves between devices by JAX's collectives and lax.ppermute only.
A program may use at most 128 MiB of HBM per device.

```python
import math
import jax
import jax.numpy as jnp
from jax import lax

NFFT = 256
HOP = 128
NF = 2
NT = 4096
NGRID = 65536
NB = 32


def draw_snapshots(key, part):
    keys = jax.random.split(jax.random.fold_in(key, 17), 2)
    position = jnp.arange(NGRID, dtype=jnp.float32) / NGRID
    rough = jnp.exp(jax.random.uniform(keys[1], (NGRID,), jnp.float32, 0.0, math.log(10.0)))
    amplitude = jnp.power(3.0, position) * rough / 8.0
    noise = jnp.clip(jax.random.normal(keys[0], (NT, NGRID), jnp.float32), -5.0, 5.0)
    values = noise * amplitude[None, :]
    return jnp.clip(values, -24.0, 24.0).astype(jnp.bfloat16)


def setup_inputs(seed: int = 0) -> dict:
    arg_keys = jax.random.split(jax.random.key(seed), 3)
    snapshots = draw_snapshots(jax.random.fold_in(arg_keys[2], 71), 0)
    freq_bins = jax.random.randint(arg_keys[1], (NF,), 1, HOP).astype(jnp.int32)
    return dict(snapshots=snapshots, freq_bins=freq_bins)


ridge_term = 0.01

def make_table(freq_bins):
    sample = jnp.arange(NFFT, dtype=jnp.int32)
    sample_f = sample.astype(jnp.float32)
    hann_taper = 0.5 - 0.5 * jnp.cos(2.0 * jnp.pi * sample_f / NFFT)
    window = hann_taper / jnp.sqrt(jnp.sum(hann_taper * hann_taper))
    phase_idx = freq_bins[:, None] * sample[None, :] % NFFT
    angles = 2.0 * jnp.pi * phase_idx.astype(jnp.float32) / NFFT
    table = jnp.stack([window * jnp.cos(angles), -window * jnp.sin(angles)], axis=1)
    return table.astype(jnp.bfloat16)

def reference(snapshots, freq_bins):
    table_rows = make_table(freq_bins).astype(jnp.float32).reshape(NF * 2, NFFT)
    halves = snapshots.reshape(NB, HOP, NGRID)

    def one_block(block_idx):
        first = lax.dynamic_index_in_dim(halves, block_idx, 0, keepdims=False).astype(jnp.float32)
        second = lax.dynamic_index_in_dim(halves, (block_idx + 1) % NB, 0, keepdims=False).astype(jnp.float32)
        lead_part = jnp.dot(table_rows[:, :HOP].astype(jnp.float32), first.astype(jnp.float32), precision=lax.Precision.HIGHEST, preferred_element_type=jnp.float32)
        trail_part = jnp.dot(table_rows[:, HOP:].astype(jnp.float32), second.astype(jnp.float32), precision=lax.Precision.HIGHEST, preferred_element_type=jnp.float32)
        return lead_part + trail_part
    stacked = lax.map(one_block, jnp.arange(NB, dtype=jnp.int32))
    coeffs = jnp.transpose(stacked, (1, 0, 2)).reshape(NF, 2 * NB, NGRID)
    gram_matrix = jnp.einsum('fcp,fdp->fcd', coeffs, coeffs, precision=lax.Precision.HIGHEST) / NGRID
    identity = jnp.eye(2 * NB, dtype=gram_matrix.dtype)
    factor = jnp.linalg.cholesky(gram_matrix + ridge_term * identity[None])
    whitened = lax.linalg.triangular_solve(factor, coeffs, left_side=True, lower=True)
    return (gram_matrix, whitened)
```

```python
import math

import jax
import jax.numpy as jnp
import numpy as np
from jax import lax
from jax.experimental import pallas as pl
from jax.experimental.pallas import tpu as pltpu
from jax.sharding import PartitionSpec as P

NFFT = 256
HOP = 128
NF = 2
SERIES = 2 * NF
SUB = 8

ridge_term = 0.01


def window_norm():
    sample = np.arange(NFFT, dtype=np.float64)
    taper = 0.5 - 0.5 * np.cos(2.0 * np.pi * sample / NFFT)
    return float(np.sqrt(np.sum(taper * taper)))


def fill_table(freq_ref, shape, half_count):
    row = lax.broadcasted_iota(jnp.int32, shape, 0)
    col = lax.broadcasted_iota(jnp.int32, shape, 1)
    group = row // SERIES
    series = row % SERIES
    block = jnp.where(group == half_count, -1, group)
    half = col // HOP
    trailing = half == block + 1
    leading = half == block
    sample = col % HOP + jnp.where(trailing, HOP, 0)
    bins = jnp.where(series // 2 == 0, freq_ref[0], freq_ref[1])
    phase = (bins * sample + jnp.where(series % 2 == 1, NFFT // 4, 0)) % NFFT
    step = 2.0 * math.pi / NFFT
    taper = 0.5 - 0.5 * jnp.cos(step * sample.astype(jnp.float32))
    wave = jnp.cos(step * phase.astype(jnp.float32))
    value = taper * (1.0 / window_norm()) * wave
    used = (trailing | leading) & (group <= half_count)
    return jnp.where(used, value, 0.0).astype(jnp.bfloat16)


def block_sums(freq_bins, snapshots, shards):
    samples, points = snapshots.shape
    half_count = samples // HOP
    rows = SERIES * half_count
    width = points // shards
    fold = width // half_count
    table_rows = rows + SUB * 2

    def body(freq_ref, data_ref, out_ref, table_ref):
        @pl.when(pl.program_id(0) == 0)
        def _():
            table_ref[...] = fill_table(freq_ref, table_ref.shape, half_count)

        sums = jnp.dot(table_ref[...], data_ref[...], preferred_element_type=jnp.float32)
        out_ref[0, :, :width] = sums[:rows].astype(jnp.bfloat16)
        early = sums[rows : rows + SERIES]
        folded = jnp.concatenate(
            [early[:, k * fold : (k + 1) * fold] for k in range(half_count)], axis=0
        )
        out_ref[0, :, width:] = folded.astype(jnp.bfloat16)

    return pl.pallas_call(
        body,
        grid=(shards,),
        in_specs=[
            pl.BlockSpec(memory_space=pltpu.SMEM),
            pl.BlockSpec((samples, width), lambda d: (0, d)),
        ],
        out_specs=pl.BlockSpec((1, rows, width + fold), lambda d: (d, 0, 0)),
        out_shape=jax.ShapeDtypeStruct((shards, rows, width + fold), jnp.bfloat16),
        scratch_shapes=[pltpu.VMEM((table_rows, samples), jnp.bfloat16)],
        name="block_sums",
    )(freq_bins, snapshots)


def join_matrix(shards, half_count):
    rows = SERIES * half_count
    block_count = shards * half_count
    out = np.zeros((half_count, SERIES * block_count, 2 * shards * rows), np.float32)
    for k in range(half_count):
        for series in range(SERIES):
            for shard in range(shards):
                for j in range(half_count):
                    target = series * block_count + shard * half_count + j
                    out[k, target, shard * rows + j * SERIES + series] = 1.0
                    if j == half_count - 1:
                        after = (shard + 1) % shards
                        out[k, target, (shards + after) * rows + k * SERIES + series] = 1.0
    return jnp.asarray(out, jnp.bfloat16)


def join_and_gram(received, half_count, grid_total):
    shards, rows, span = received.shape
    width = span * half_count // (half_count + 1)
    fold = width // half_count
    total = shards * rows
    size = total // NF

    def body(join_ref, data_ref, columns_ref, gram_ref):
        folded = data_ref[:, :, width:].reshape(total, fold)
        for k in range(half_count):
            own = data_ref[:, :, k * fold : (k + 1) * fold].reshape(total, fold)
            both = jnp.concatenate([own, folded], axis=0)
            joined = jnp.dot(join_ref[k], both, preferred_element_type=jnp.float32)
            columns_ref[:, k * fold : (k + 1) * fold] = joined.astype(jnp.bfloat16)
        columns = columns_ref[...]
        products = lax.dot_general(
            columns, columns, (((1,), (1,)), ((), ())), preferred_element_type=jnp.float32
        )
        for f in range(NF):
            part = products[f * size : (f + 1) * size, f * size : (f + 1) * size]
            gram_ref[:, f * size : (f + 1) * size] = part * (1.0 / grid_total)

    return pl.pallas_call(
        body,
        out_shape=(
            jax.ShapeDtypeStruct((total, width), jnp.bfloat16),
            jax.ShapeDtypeStruct((size, NF * size), jnp.float32),
        ),
        name="join_and_gram",
    )(join_matrix(shards, half_count), received)


def exchange_sum(value, axis):
    devices = lax.axis_size(axis)
    step = 1
    while step < devices:
        value = value + lax.ppermute(value, axis, [(i, i ^ step) for i in range(devices)])
        step *= 2
    return value


def inverse_factor(gram_ref, work_ref, inverse_ref, size):
    lanes = NF * size
    row = lax.broadcasted_iota(jnp.int32, (size, lanes), 0)
    lane = lax.broadcasted_iota(jnp.int32, (size, lanes), 1) % size
    eye = jnp.where(row == lane, 1.0, 0.0)
    work_ref[...] = gram_ref[...] + ridge_term * eye
    inverse_ref[...] = eye
    sub = lax.broadcasted_iota(jnp.int32, (SUB, lanes), 0)
    for start in range(0, size, SUB):
        stop = start + SUB
        left = work_ref[start:, :]
        columns = []
        for m in range(SUB):
            columns.append(
                jnp.concatenate(
                    [
                        jnp.broadcast_to(
                            left[:, f * size + start + m : f * size + start + m + 1],
                            (size - start, size),
                        )
                        for f in range(NF)
                    ],
                    axis=1,
                )
            )

        def spread(array, i):
            return jnp.broadcast_to(array[i : i + 1, :], (SUB, lanes))

        d = [[spread(columns[j], i) for j in range(i + 1)] for i in range(SUB)]
        low = [[None] * SUB for _ in range(SUB)]
        for k in range(SUB):
            scale = lax.rsqrt(d[k][k])
            for j in range(k):
                low[k][j] = low[k][j] * scale
            low[k][k] = scale
            below = [d[i][k] * scale for i in range(k + 1, SUB)]
            for i in range(k + 1, SUB):
                x = below[i - k - 1]
                for j in range(k + 1, i + 1):
                    d[i][j] = d[i][j] - x * below[j - k - 1]
                for j in range(k + 1):
                    term = x * low[k][j]
                    low[i][j] = -term if low[i][j] is None else low[i][j] - term
        top = work_ref[start:stop, :]
        side = inverse_ref[start:stop, :]

        def solve_rows(block):
            source = [spread(block, m) for m in range(SUB)]
            solved = []
            for j in range(SUB):
                acc = low[j][0] * source[0]
                for m in range(1, j + 1):
                    acc = acc + low[j][m] * source[m]
                solved.append(acc)
            return solved

        def apply_transposed(solved):
            out = []
            for m in range(SUB):
                acc = low[m][m] * solved[m]
                for j in range(m + 1, SUB):
                    acc = acc + low[j][m] * solved[j]
                out.append(acc)
            return out

        solved_side = solve_rows(side)
        packed = solved_side[0]
        for j in range(1, SUB):
            packed = jnp.where(sub == j, solved_side[j], packed)
        inverse_ref[start:stop, :] = packed
        if stop < size:
            weights_top = apply_transposed(solve_rows(top))
            weights_side = apply_transposed(solved_side)
            for first in range(stop, size, SUB):
                rest = work_ref[first : first + SUB, :]
                rest_side = inverse_ref[first : first + SUB, :]
                for m in range(SUB):
                    column = columns[m][first - start : first - start + SUB]
                    rest = rest - column * weights_top[m]
                    rest_side = rest_side - column * weights_side[m]
                work_ref[first : first + SUB, :] = rest
                inverse_ref[first : first + SUB, :] = rest_side


def whiten(gram, columns):
    size = gram.shape[0]
    total, width = columns.shape
    chunk = min(width, 512)

    def body(gram_ref, columns_ref, gram_out, white_ref, work_ref, inverse_ref, left_ref):
        for f in range(NF):
            gram_out[f] = gram_ref[:, f * size : (f + 1) * size]
        inverse_factor(gram_ref, work_ref, inverse_ref, size)
        lane = lax.broadcasted_iota(jnp.int32, (size, NF * size), 1)
        for f in range(NF):
            own = jnp.where(lane // size == f, inverse_ref[...], 0.0)
            high = own.astype(jnp.bfloat16)
            rest = (own - high.astype(jnp.float32)).astype(jnp.bfloat16)
            left_ref[f * size : (f + 1) * size, : NF * size] = high
            left_ref[f * size : (f + 1) * size, NF * size :] = rest
        for first in range(0, width, chunk):
            part = columns_ref[:, first : first + chunk]
            both = jnp.concatenate([part, part], axis=0)
            done = jnp.dot(left_ref[...], both, preferred_element_type=jnp.float32)
            for f in range(NF):
                white_ref[f, :, first : first + chunk] = done[f * size : (f + 1) * size]

    return pl.pallas_call(
        body,
        out_shape=(
            jax.ShapeDtypeStruct((NF, size, size), jnp.float32),
            jax.ShapeDtypeStruct((NF, size, width), jnp.float32),
        ),
        scratch_shapes=[
            pltpu.VMEM((size, NF * size), jnp.float32),
            pltpu.VMEM((size, NF * size), jnp.float32),
            pltpu.VMEM((total, 2 * NF * size), jnp.bfloat16),
        ],
        name="whiten",
    )(gram, columns)


def on_device(snapshots, freq_bins):
    shards = lax.axis_size("tm")
    half_count = snapshots.shape[0] // HOP
    grid_total = snapshots.shape[1] * lax.axis_size("space")
    parts = block_sums(freq_bins, snapshots, shards)
    received = lax.all_to_all(parts, "tm", 0, 0, tiled=True)
    columns, gram = join_and_gram(received, half_count, grid_total)
    gram = exchange_sum(exchange_sum(gram, "space"), "tm")
    return whiten(gram, columns)


def solution(mesh):
    placed = (P("tm", "space"), P())
    return jax.shard_map(
        on_device,
        mesh=mesh,
        in_specs=placed,
        out_specs=(P(), P(None, None, ("space", "tm"))),
        check_vma=False,
    )
```

```python
import math

import jax
import jax.numpy as jnp
import numpy as np
from jax import lax
from jax.experimental import pallas as pl
from jax.experimental.pallas import tpu as pltpu
from jax.sharding import PartitionSpec as P

NFFT = 256
HOP = 128
NF = 2
SERIES = 2 * NF
SUB = 8

ridge_term = 0.01


def window_norm():
    sample = np.arange(NFFT, dtype=np.float64)
    taper = 0.5 - 0.5 * np.cos(2.0 * np.pi * sample / NFFT)
    return float(np.sqrt(np.sum(taper * taper)))


def fill_table(freq_ref, shape, half_count):
    row = lax.broadcasted_iota(jnp.int32, shape, 0)
    col = lax.broadcasted_iota(jnp.int32, shape, 1)
    group = row // SERIES
    series = row % SERIES
    block = jnp.where(group == half_count, -1, group)
    half = col // HOP
    trailing = half == block + 1
    leading = half == block
    sample = col % HOP + jnp.where(trailing, HOP, 0)
    bins = jnp.where(series // 2 == 0, freq_ref[0], freq_ref[1])
    phase = (bins * sample + jnp.where(series % 2 == 1, NFFT // 4, 0)) % NFFT
    step = 2.0 * math.pi / NFFT
    taper = 0.5 - 0.5 * jnp.cos(step * sample.astype(jnp.float32))
    wave = jnp.cos(step * phase.astype(jnp.float32))
    value = taper * (1.0 / window_norm()) * wave
    used = (trailing | leading) & (group <= half_count)
    return jnp.where(used, value, 0.0).astype(jnp.bfloat16)


def block_sums(freq_bins, position, snapshots, shards, shifts):
    samples, points = snapshots.shape
    half_count = samples // HOP
    rows = SERIES * half_count
    width = points // shards
    fold = width // half_count
    table_rows = rows + SUB * 2
    count = len(shifts)

    def body(freq_ref, position_ref, data_ref, *refs):
        outs, (join_ref, table_ref, buffer_ref, sems) = refs[:count], refs[count:]
        copies = []
        for i, shift in enumerate(shifts):
            target = (position_ref[0] + shift) % shards
            first = pl.multiple_of(target * width, width)
            copies.append(
                pltpu.make_async_copy(
                    data_ref.at[:, pl.ds(first, width)], buffer_ref.at[i], sems.at[i]
                )
            )
            copies[-1].start()
        table_ref[...] = fill_table(freq_ref, table_ref.shape, half_count)
        for k in range(half_count):
            join_ref[k] = join_matrix(position_ref[0], shifts, k, half_count)
        for copy, out_ref, i in zip(copies, outs, range(count)):
            copy.wait()
            sums = jnp.dot(table_ref[...], buffer_ref[i], preferred_element_type=jnp.float32)
            out_ref[:, :width] = sums[:rows].astype(jnp.bfloat16)
            early = sums[rows : rows + SERIES]
            folded = jnp.concatenate(
                [early[:, k * fold : (k + 1) * fold] for k in range(half_count)], axis=0
            )
            out_ref[:, width:] = folded.astype(jnp.bfloat16)

    return pl.pallas_call(
        body,
        in_specs=[
            pl.BlockSpec(memory_space=pltpu.SMEM),
            pl.BlockSpec(memory_space=pltpu.SMEM),
            pl.BlockSpec(memory_space=pl.ANY),
        ],
        out_shape=tuple(pltpu.VMEM((rows, width + fold), jnp.bfloat16) for _ in shifts)
        + (pltpu.VMEM((half_count, rows * shards, 2 * rows * shards), jnp.bfloat16),),
        out_specs=tuple([pl.BlockSpec(memory_space=pltpu.VMEM)] * (count + 1)),
        scratch_shapes=[
            pltpu.VMEM((table_rows, samples), jnp.bfloat16),
            pltpu.VMEM((count, samples, width), jnp.bfloat16),
            pltpu.SemaphoreType.DMA((count,)),
        ],
        name="block_sums",
    )(freq_bins, position, snapshots)


def join_matrix(position, shifts, k, half_count):
    shards = len(shifts)
    rows = SERIES * half_count
    total = shards * rows
    target = lax.broadcasted_iota(jnp.int32, (total, 1), 0)
    series = target // (shards * half_count)
    shard = target // half_count % shards
    block = target % half_count
    source = lax.broadcasted_iota(jnp.int32, (1, 2 * total), 1)
    slot, row = source // rows % shards, source % rows
    sender = jnp.zeros_like(source)
    for i, shift in enumerate(shifts):
        sender = jnp.where(slot == i, (position - shift + shards) % shards, sender)
    folded = source >= total
    code = jnp.where(folded, total, 0) + sender * rows + row
    own = shard * rows + block * SERIES + series
    after = (shard + 1) % shards
    early = total + after * rows + k * SERIES + series
    early = jnp.where(block == half_count - 1, early, -1)
    return jnp.where((code == own) | (code == early), 1.0, 0.0).astype(jnp.bfloat16)


def join_and_gram(received, joins, half_count, grid_total):
    shards = len(received)
    rows, span = received[0].shape
    width = span * half_count // (half_count + 1)
    fold = width // half_count
    total = shards * rows
    size = total // NF

    def body(join_ref, *refs):
        parts, (columns_ref, gram_ref) = refs[:shards], refs[shards:]
        folded = [part[:, width:] for part in parts]
        for k in range(half_count):
            own = [part[:, k * fold : (k + 1) * fold] for part in parts]
            both = jnp.concatenate(own + folded, axis=0)
            joined = jnp.dot(join_ref[k], both, preferred_element_type=jnp.float32)
            columns_ref[:, k * fold : (k + 1) * fold] = joined.astype(jnp.bfloat16)
        columns = columns_ref[...]
        products = lax.dot_general(
            columns, columns, (((1,), (1,)), ((), ())), preferred_element_type=jnp.float32
        )
        for f in range(NF):
            part = products[f * size : (f + 1) * size, f * size : (f + 1) * size]
            gram_ref[:, f * size : (f + 1) * size] = part * (1.0 / grid_total)

    return pl.pallas_call(
        body,
        in_specs=[pl.BlockSpec(memory_space=pltpu.VMEM)] * (shards + 1),
        out_shape=(
            pltpu.VMEM((total, width), jnp.bfloat16),
            pltpu.VMEM((size, NF * size), jnp.float32),
        ),
        out_specs=(pl.BlockSpec(memory_space=pltpu.VMEM),) * 2,
        name="join_and_gram",
    )(near(joins), *[near(part) for part in received])


def near(value):
    return pltpu.with_memory_space_constraint(value, pltpu.VMEM)


GRID = ("space", "tm")


def swapped(value, flips):
    wide, long = (lax.axis_size(name) for name in GRID)
    pairs = [
        (i * long + j, (i ^ flips[0]) * long + (j ^ flips[1]))
        for i in range(wide)
        for j in range(long)
    ]
    return lax.ppermute(value, GRID, pairs)


def exchange_rounds():
    bits = [(1 << k, 0) for k in range((lax.axis_size("space") - 1).bit_length())]
    bits += [(0, 1 << k) for k in range((lax.axis_size("tm") - 1).bit_length())]
    rounds, rest = [bits[:1]], bits[1:]
    while rest:
        rounds.append(rest[:2])
        rest = rest[2:]
    return rounds


def peers_of(value, bits):
    if len(bits) == 1:
        return [swapped(value, bits[0])]
    (a, b), (c, d) = bits
    return [swapped(value, flips) for flips in ((a, b), (c, d), (a + c, b + d))]


def add_up(values):
    while len(values) > 1:
        values = [values[i] + values[i + 1] for i in range(0, len(values), 2)]
    return values[0]


def inverse_factor(gram_ref, work_ref, inverse_ref, size):
    lanes = NF * size
    row = lax.broadcasted_iota(jnp.int32, (size, lanes), 0)
    lane = lax.broadcasted_iota(jnp.int32, (size, lanes), 1) % size
    eye = jnp.where(row == lane, 1.0, 0.0)
    work_ref[...] = gram_ref[...] + ridge_term * eye
    inverse_ref[...] = eye
    sub = lax.broadcasted_iota(jnp.int32, (SUB, lanes), 0)
    for start in range(0, size, SUB):
        stop = start + SUB
        left = work_ref[start:, :]
        columns = []
        for m in range(SUB):
            columns.append(
                jnp.concatenate(
                    [
                        jnp.broadcast_to(
                            left[:, f * size + start + m : f * size + start + m + 1],
                            (size - start, size),
                        )
                        for f in range(NF)
                    ],
                    axis=1,
                )
            )

        def spread(array, i):
            return jnp.broadcast_to(array[i : i + 1, :], (SUB, lanes))

        d = [[spread(columns[j], i) for j in range(i + 1)] for i in range(SUB)]
        low = [[None] * SUB for _ in range(SUB)]
        for k in range(SUB):
            scale = lax.rsqrt(d[k][k])
            for j in range(k):
                low[k][j] = low[k][j] * scale
            low[k][k] = scale
            below = [d[i][k] * scale for i in range(k + 1, SUB)]
            for i in range(k + 1, SUB):
                x = below[i - k - 1]
                for j in range(k + 1, i + 1):
                    d[i][j] = d[i][j] - x * below[j - k - 1]
                for j in range(k + 1):
                    term = x * low[k][j]
                    low[i][j] = -term if low[i][j] is None else low[i][j] - term
        top = work_ref[start:stop, :]
        side = inverse_ref[start:stop, :]

        def solve_rows(block):
            source = [spread(block, m) for m in range(SUB)]
            solved = []
            for j in range(SUB):
                acc = low[j][0] * source[0]
                for m in range(1, j + 1):
                    acc = acc + low[j][m] * source[m]
                solved.append(acc)
            return solved

        def apply_transposed(solved):
            out = []
            for m in range(SUB):
                acc = low[m][m] * solved[m]
                for j in range(m + 1, SUB):
                    acc = acc + low[j][m] * solved[j]
                out.append(acc)
            return out

        solved_side = solve_rows(side)
        packed = solved_side[0]
        for j in range(1, SUB):
            packed = jnp.where(sub == j, solved_side[j], packed)
        inverse_ref[start:stop, :] = packed
        if stop < size:
            weights_top = apply_transposed(solve_rows(top))
            weights_side = apply_transposed(solved_side)
            for first in range(stop, size, SUB):
                rest = work_ref[first : first + SUB, :]
                rest_side = inverse_ref[first : first + SUB, :]
                for m in range(SUB):
                    column = columns[m][first - start : first - start + SUB]
                    rest = rest - column * weights_top[m]
                    rest_side = rest_side - column * weights_side[m]
                work_ref[first : first + SUB, :] = rest
                inverse_ref[first : first + SUB, :] = rest_side


def whiten(grams, columns):
    count = len(grams)
    size = grams[0].shape[0]
    total, width = columns.shape
    chunk = min(width, 512)

    def body(*refs):
        columns_ref, gram_out, white_ref, gram_ref, work_ref, inverse_ref, left_ref = refs[count:]
        gram_ref[...] = add_up([ref[...] for ref in refs[:count]])
        for f in range(NF):
            gram_out[f] = gram_ref[:, f * size : (f + 1) * size]
        inverse_factor(gram_ref, work_ref, inverse_ref, size)
        lane = lax.broadcasted_iota(jnp.int32, (size, NF * size), 1)
        for f in range(NF):
            own = jnp.where(lane // size == f, inverse_ref[...], 0.0)
            high = own.astype(jnp.bfloat16)
            rest = (own - high.astype(jnp.float32)).astype(jnp.bfloat16)
            left_ref[f * size : (f + 1) * size, : NF * size] = high
            left_ref[f * size : (f + 1) * size, NF * size :] = rest
        for first in range(0, width, chunk):
            part = columns_ref[:, first : first + chunk]
            both = jnp.concatenate([part, part], axis=0)
            done = jnp.dot(left_ref[...], both, preferred_element_type=jnp.float32)
            for f in range(NF):
                white_ref[f, :, first : first + chunk] = done[f * size : (f + 1) * size]

    return pl.pallas_call(
        body,
        in_specs=[pl.BlockSpec(memory_space=pltpu.VMEM)] * (count + 1),
        out_shape=(
            jax.ShapeDtypeStruct((NF, size, size), jnp.float32),
            jax.ShapeDtypeStruct((NF, size, width), jnp.float32),
        ),
        scratch_shapes=[
            pltpu.VMEM((size, NF * size), jnp.float32),
            pltpu.VMEM((size, NF * size), jnp.float32),
            pltpu.VMEM((size, NF * size), jnp.float32),
            pltpu.VMEM((total, 2 * NF * size), jnp.bfloat16),
        ],
        name="whiten",
    )(*[near(gram) for gram in grams], near(columns))


def on_device(snapshots, freq_bins):
    shards = lax.axis_size("tm")
    half_count = snapshots.shape[0] // HOP
    grid_total = snapshots.shape[1] * lax.axis_size("space")
    position = lax.axis_index("tm").astype(jnp.int32)[None]
    shifts = sorted(range(shards), key=lambda k: abs(k - shards // 2))
    *parts, joins = block_sums(freq_bins, position, snapshots, shards, shifts)
    received = []
    for shift, part in zip(shifts, parts):
        pairs = [(i, (i + shift) % shards) for i in range(shards)]
        received.append(lax.ppermute(part, "tm", pairs) if shift else part)
    columns, gram = join_and_gram(received, joins, half_count, grid_total)
    grams = [gram]
    for bits in exchange_rounds():
        gram = add_up(grams)
        grams = [gram] + peers_of(gram, bits)
    return whiten(grams, columns)


def solution(mesh):
    placed = (P("tm", "space"), P())
    return jax.shard_map(
        on_device,
        mesh=mesh,
        in_specs=placed,
        out_specs=(P(), P(None, None, ("space", "tm"))),
        check_vma=False,
    )
```

```python
import math

import jax
import jax.numpy as jnp
import numpy as np
from jax import lax
from jax.experimental import pallas as pl
from jax.experimental.pallas import tpu as pltpu
from jax.sharding import PartitionSpec as P

NFFT = 256
HOP = 128
NF = 2
SERIES = 2 * NF
SUB = 8

ridge_term = 0.01


def window_norm():
    sample = np.arange(NFFT, dtype=np.float64)
    taper = 0.5 - 0.5 * np.cos(2.0 * np.pi * sample / NFFT)
    return float(np.sqrt(np.sum(taper * taper)))


def fill_table(freq_ref, table_ref, half_count):
    row = lax.broadcasted_iota(jnp.int32, (SUB, NFFT), 0)
    sample = lax.broadcasted_iota(jnp.int32, (SUB, NFFT), 1)
    series = row % SERIES
    bins = jnp.where(series // 2 == 0, freq_ref[0], freq_ref[1])
    phase = (bins * sample + jnp.where(series % 2 == 1, NFFT // 4, 0)) % NFFT
    step = 2.0 * math.pi / NFFT
    taper = 0.5 - 0.5 * jnp.cos(step * sample.astype(jnp.float32))
    value = taper * (1.0 / window_norm()) * jnp.cos(step * phase.astype(jnp.float32))
    leading, trailing = value[:, :HOP], value[:, HOP:]
    group_of = lax.broadcasted_iota(jnp.int32, (SUB, HOP), 0) // SERIES
    per_tile = SUB // SERIES
    for first in range(0, table_ref.shape[0], 2 * SUB):
        for half in range(half_count):
            tiles = []
            for start in (first // SERIES, first // SERIES + per_tile):
                group = group_of + start
                block = jnp.where(group == half_count, -1, group)
                tile = jnp.where(half == block, leading, 0.0)
                tile = jnp.where(half == block + 1, trailing, tile)
                tiles.append(jnp.where(group > half_count, 0.0, tile))
            packed = jnp.concatenate(tiles, axis=0).astype(jnp.bfloat16)
            table_ref[first : first + 2 * SUB, half * HOP : (half + 1) * HOP] = packed


def block_sums(freq_bins, position, snapshots, shards, shifts):
    samples, points = snapshots.shape
    half_count = samples // HOP
    rows = SERIES * half_count
    width = points // shards
    fold = width // half_count
    table_shape = (rows + SUB * 2, samples)
    count = len(shifts)

    def body(freq_ref, position_ref, data_ref, *refs):
        outs, (join_ref, table_ref, buffer_ref, sems) = refs[:count], refs[count:]
        copies = []
        for i, shift in enumerate(shifts):
            first = pl.multiple_of((position_ref[0] ^ shift) * width, width)
            copies.append(
                pltpu.make_async_copy(
                    data_ref.at[:, pl.ds(first, width)], buffer_ref.at[i], sems.at[i]
                )
            )
            copies[-1].start()
        fill_table(freq_ref, table_ref, half_count)
        for k in range(half_count):
            join_ref[k] = join_matrix(position_ref[0], shifts, k, half_count)
        for copy, out_ref, i in zip(copies, outs, range(count)):
            copy.wait()
            sums = jnp.dot(table_ref[...], buffer_ref[i], preferred_element_type=jnp.float32)
            out_ref[:, :width] = sums[:rows].astype(jnp.bfloat16)
            early = sums[rows : rows + SERIES]
            folded = jnp.concatenate(
                [early[:, k * fold : (k + 1) * fold] for k in range(half_count)], axis=0
            )
            out_ref[:, width:] = folded.astype(jnp.bfloat16)

    local = pl.BlockSpec(memory_space=pltpu.VMEM)
    shapes = [pltpu.VMEM((rows, width + fold), jnp.bfloat16) for _ in shifts]
    shapes.append(pltpu.VMEM((half_count, rows * shards, 2 * rows * shards), jnp.bfloat16))
    smem = pl.BlockSpec(memory_space=pltpu.SMEM)
    return pl.pallas_call(
        body,
        in_specs=[smem, smem, pl.BlockSpec(memory_space=pl.ANY)],
        out_shape=tuple(shapes),
        out_specs=(local,) * len(shapes),
        scratch_shapes=[
            pltpu.VMEM(table_shape, jnp.bfloat16),
            pltpu.VMEM((count, samples, width), jnp.bfloat16),
            pltpu.SemaphoreType.DMA((count,)),
        ],
        name="block_sums",
    )(freq_bins, position, snapshots)


def join_matrix(position, shifts, k, half_count):
    shards = len(shifts)
    rows = SERIES * half_count
    total = shards * rows
    target = lax.broadcasted_iota(jnp.int32, (total, 1), 0)
    series = target // (shards * half_count)
    shard = target // half_count % shards
    block = target % half_count
    source = lax.broadcasted_iota(jnp.int32, (1, 2 * total), 1)
    slot, row = source // rows % shards, source % rows
    sender = jnp.zeros_like(source)
    for i, shift in enumerate(shifts):
        sender = jnp.where(slot == i, position ^ shift, sender)
    folded = source >= total
    code = jnp.where(folded, total, 0) + sender * rows + row
    own = shard * rows + block * SERIES + series
    after = (shard + 1) % shards
    early = total + after * rows + k * SERIES + series
    early = jnp.where(block == half_count - 1, early, -1)
    return jnp.where((code == own) | (code == early), 1.0, 0.0).astype(jnp.bfloat16)


def join_and_gram(received, joins, half_count, grid_total):
    shards = len(received)
    rows, span = received[0].shape
    width = span * half_count // (half_count + 1)
    fold = width // half_count
    total = shards * rows
    size = total // NF

    def body(join_ref, *refs):
        parts, (columns_ref, gram_ref) = refs[:shards], refs[shards:]
        folded = [part[:, width:] for part in parts]
        for k in range(half_count):
            own = [part[:, k * fold : (k + 1) * fold] for part in parts]
            both = jnp.concatenate(own + folded, axis=0)
            joined = jnp.dot(join_ref[k], both, preferred_element_type=jnp.float32)
            columns_ref[:, k * fold : (k + 1) * fold] = joined.astype(jnp.bfloat16)
        columns = columns_ref[...]
        products = lax.dot_general(
            columns, columns, (((1,), (1,)), ((), ())), preferred_element_type=jnp.float32
        )
        for f in range(NF):
            part = products[f * size : (f + 1) * size, f * size : (f + 1) * size]
            gram_ref[:, f * size : (f + 1) * size] = part * (1.0 / grid_total)

    return pl.pallas_call(
        body,
        in_specs=[pl.BlockSpec(memory_space=pltpu.VMEM)] * (shards + 1),
        out_shape=(
            pltpu.VMEM((total, width), jnp.bfloat16),
            pltpu.VMEM((size, NF * size), jnp.float32),
        ),
        out_specs=(pl.BlockSpec(memory_space=pltpu.VMEM),) * 2,
        name="join_and_gram",
    )(near(joins), *[near(part) for part in received])


def near(value):
    return pltpu.with_memory_space_constraint(value, pltpu.VMEM)


def spread_order(shards):
    bits = (shards - 1).bit_length()
    order = [int(f"{k:0{bits}b}"[::-1], 2) for k in range(1, shards)]
    return order + [0]


GRID = ("space", "tm")


def swapped(value, flips):
    wide, long = (lax.axis_size(name) for name in GRID)
    pairs = [
        (i * long + j, (i ^ flips[0]) * long + (j ^ flips[1]))
        for i in range(wide)
        for j in range(long)
    ]
    return lax.ppermute(value, GRID, pairs)


def exchange_rounds():
    bits = [(1 << k, 0) for k in range((lax.axis_size("space") - 1).bit_length())]
    bits += [(0, 1 << k) for k in range((lax.axis_size("tm") - 1).bit_length())]
    rounds, rest = [bits[:1]], bits[1:]
    while rest:
        rounds.append(rest[:2])
        rest = rest[2:]
    return rounds


def peers_of(value, bits):
    if len(bits) == 1:
        return [swapped(value, bits[0])]
    (a, b), (c, d) = bits
    return [swapped(value, flips) for flips in ((a, b), (c, d), (a + c, b + d))]


def add_up(values):
    while len(values) > 1:
        values = [values[i] + values[i + 1] for i in range(0, len(values), 2)]
    return values[0]


def spread_row(block, i):
    return jnp.broadcast_to(block[i : i + 1, :], block.shape)


def block_inverse(d):
    low = [[None] * SUB for _ in range(SUB)]
    for k in range(SUB):
        scale = lax.rsqrt(d[k][k])
        for j in range(k):
            low[k][j] = low[k][j] * scale
        low[k][k] = scale
        below = [d[i][k] * scale for i in range(k + 1, SUB)]
        for i in range(k + 1, SUB):
            x = below[i - k - 1]
            for j in range(k + 1, i + 1):
                d[i][j] = d[i][j] - x * below[j - k - 1]
            for j in range(k + 1):
                term = x * low[k][j]
                low[i][j] = -term if low[i][j] is None else low[i][j] - term
    return low


def tree_sum(terms):
    while len(terms) > 1:
        pairs = [terms[i] + terms[i + 1] for i in range(0, len(terms) - 1, 2)]
        terms = pairs + terms[len(pairs) * 2 :]
    return terms[0]


def inverse_factor(gram, size):
    lanes = NF * size
    sub = lax.broadcasted_iota(jnp.int32, (SUB, lanes), 0)
    lane = lax.broadcasted_iota(jnp.int32, (SUB, lanes), 1)
    work, side = [], []
    for start in range(0, size, SUB):
        eye = jnp.where(lane % size == sub + start, 1.0, 0.0)
        work.append(gram[start : start + SUB, :] + ridge_term * eye)
        side.append(eye)
    done = []
    for step in range(size // SUB):
        start = step * SUB

        def column_of(block, m):
            first = jnp.broadcast_to(block[:, start + m : start + m + 1], (SUB, lanes))
            for f in range(1, NF):
                at = f * size + start + m
                other = jnp.broadcast_to(block[:, at : at + 1], (SUB, lanes))
                first = jnp.where(lane < f * size, first, other)
            return first

        columns = [[column_of(block, m) for m in range(SUB)] for block in work]
        head = columns[0]
        low = block_inverse(
            [[spread_row(head[j], i) for j in range(i + 1)] for i in range(SUB)]
        )

        def solve_rows(block):
            source = [spread_row(block, m) for m in range(SUB)]
            return [
                tree_sum([low[j][m] * source[m] for m in range(j + 1)]) for j in range(SUB)
            ]

        def apply_transposed(solved):
            return [
                tree_sum([low[j][m] * solved[j] for j in range(m, SUB)]) for m in range(SUB)
            ]

        solved_side = solve_rows(side[0])
        packed = solved_side[0]
        for j in range(1, SUB):
            packed = jnp.where(sub == j, solved_side[j], packed)
        done.append(packed)
        if len(work) > 1:
            top = apply_transposed(solve_rows(work[0]))
            top_side = apply_transposed(solved_side)
            work = [
                block - tree_sum([column[m] * top[m] for m in range(SUB)])
                for block, column in zip(work[1:], columns[1:])
            ]
            side = [
                block - tree_sum([column[m] * top_side[m] for m in range(SUB)])
                for block, column in zip(side[1:], columns[1:])
            ]
    return jnp.concatenate(done, axis=0)


def whiten(grams, columns):
    count = len(grams)
    size = grams[0].shape[0]
    total, width = columns.shape
    chunk = min(width, 512)
    chunks = width // chunk

    def body(*refs):
        columns_ref, gram_out, white_out, gram_ref, left_ref, white_ref, sems = refs[count:]
        total_gram = add_up([ref[...] for ref in refs[:count]])
        copies = []
        for f in range(NF):
            gram_ref[f] = total_gram[:, f * size : (f + 1) * size]
        copies.append(pltpu.make_async_copy(gram_ref, gram_out, sems.at[0]))
        copies[-1].start()
        inverse = inverse_factor(total_gram, size)
        lane = lax.broadcasted_iota(jnp.int32, (size, NF * size), 1)
        for f in range(NF):
            own = jnp.where(lane // size == f, inverse, 0.0)
            high = own.astype(jnp.bfloat16)
            rest = (own - high.astype(jnp.float32)).astype(jnp.bfloat16)
            left_ref[f * size : (f + 1) * size, : NF * size] = high
            left_ref[f * size : (f + 1) * size, NF * size :] = rest
        for k in range(chunks):
            here = pl.ds(k * chunk, chunk)
            part = columns_ref[:, here]
            both = jnp.concatenate([part, part], axis=0)
            done = jnp.dot(left_ref[...], both, preferred_element_type=jnp.float32)
            for f in range(NF):
                white_ref[f, :, here] = done[f * size : (f + 1) * size]
            copies.append(
                pltpu.make_async_copy(
                    white_ref.at[:, :, here], white_out.at[:, :, here], sems.at[k + 1]
                )
            )
            copies[-1].start()
        for copy in copies:
            copy.wait()

    return pl.pallas_call(
        body,
        in_specs=[pl.BlockSpec(memory_space=pltpu.VMEM)] * (count + 1),
        out_shape=(
            jax.ShapeDtypeStruct((NF, size, size), jnp.float32),
            jax.ShapeDtypeStruct((NF, size, width), jnp.float32),
        ),
        out_specs=(pl.BlockSpec(memory_space=pl.ANY),) * 2,
        scratch_shapes=[
            pltpu.VMEM((NF, size, size), jnp.float32),
            pltpu.VMEM((total, 2 * NF * size), jnp.bfloat16),
            pltpu.VMEM((NF, size, width), jnp.float32),
            pltpu.SemaphoreType.DMA((chunks + 1,)),
        ],
        name="whiten",
    )(*[near(gram) for gram in grams], near(columns))


def on_device(snapshots, freq_bins):
    shards = lax.axis_size("tm")
    half_count = snapshots.shape[0] // HOP
    grid_total = snapshots.shape[1] * lax.axis_size("space")
    position = lax.axis_index("tm").astype(jnp.int32)[None]
    shifts = spread_order(shards)
    *parts, joins = block_sums(freq_bins, position, snapshots, shards, shifts)
    received = []
    for shift, part in zip(shifts, parts):
        pairs = [(i, i ^ shift) for i in range(shards)]
        received.append(lax.ppermute(part, "tm", pairs) if shift else part)
    columns, gram = join_and_gram(received, joins, half_count, grid_total)
    grams = [gram]
    for bits in exchange_rounds():
        gram = add_up(grams)
        grams = [gram] + peers_of(gram, bits)
    return whiten(grams, columns)


def solution(mesh):
    placed = (P("tm", "space"), P())
    return jax.shard_map(
        on_device,
        mesh=mesh,
        in_specs=placed,
        out_specs=(P(), P(None, None, ("space", "tm"))),
        check_vma=False,
    )
```

```python
import math

import jax
import jax.numpy as jnp
import numpy as np
from jax import lax
from jax.experimental import pallas as pl
from jax.experimental.pallas import tpu as pltpu
from jax.sharding import PartitionSpec as P

NFFT = 256
HOP = 128
NF = 2
SERIES = 2 * NF
SUB = 8

ridge_term = 0.01


def window_norm():
    sample = np.arange(NFFT, dtype=np.float64)
    taper = 0.5 - 0.5 * np.cos(2.0 * np.pi * sample / NFFT)
    return float(np.sqrt(np.sum(taper * taper)))


def fill_table(freq_ref, table_ref, half_count):
    row = lax.broadcasted_iota(jnp.int32, (SUB, NFFT), 0)
    sample = lax.broadcasted_iota(jnp.int32, (SUB, NFFT), 1)
    series = row % SERIES
    bins = jnp.where(series // 2 == 0, freq_ref[0], freq_ref[1])
    phase = (bins * sample + jnp.where(series % 2 == 1, NFFT // 4, 0)) % NFFT
    step = 2.0 * math.pi / NFFT
    taper = 0.5 - 0.5 * jnp.cos(step * sample.astype(jnp.float32))
    value = taper * (1.0 / window_norm()) * jnp.cos(step * phase.astype(jnp.float32))
    leading, trailing = value[:, :HOP], value[:, HOP:]
    group_of = lax.broadcasted_iota(jnp.int32, (SUB, HOP), 0) // SERIES
    per_tile = SUB // SERIES
    for first in range(0, table_ref.shape[0], 2 * SUB):
        for half in range(half_count):
            tiles = []
            for start in (first // SERIES, first // SERIES + per_tile):
                group = group_of + start
                block = jnp.where(group == half_count, -1, group)
                tile = jnp.where(half == block, leading, 0.0)
                tile = jnp.where(half == block + 1, trailing, tile)
                tiles.append(jnp.where(group > half_count, 0.0, tile))
            packed = jnp.concatenate(tiles, axis=0).astype(jnp.bfloat16)
            table_ref[first : first + 2 * SUB, half * HOP : (half + 1) * HOP] = packed


def block_sums(freq_bins, position, snapshots, shards, shifts):
    samples, points = snapshots.shape
    half_count = samples // HOP
    rows = SERIES * half_count
    width = points // shards
    fold = width // half_count
    table_shape = (rows + SUB * 2, samples)
    count = len(shifts)

    def body(freq_ref, position_ref, data_ref, *refs):
        outs, (join_ref, table_ref, buffer_ref, sems) = refs[:count], refs[count:]
        copies = []
        for i, shift in enumerate(shifts):
            first = pl.multiple_of((position_ref[0] ^ shift) * width, width)
            copies.append(
                pltpu.make_async_copy(
                    data_ref.at[:, pl.ds(first, width)], buffer_ref.at[i], sems.at[i]
                )
            )
            copies[-1].start()
        fill_table(freq_ref, table_ref, half_count)
        for k in range(half_count):
            join_ref[k] = join_matrix(position_ref[0], shifts, k, half_count)
        for copy, out_ref, i in zip(copies, outs, range(count)):
            copy.wait()
            sums = jnp.dot(table_ref[...], buffer_ref[i], preferred_element_type=jnp.float32)
            out_ref[:, :width] = sums[:rows].astype(jnp.bfloat16)
            early = sums[rows : rows + SERIES]
            folded = jnp.concatenate(
                [early[:, k * fold : (k + 1) * fold] for k in range(half_count)], axis=0
            )
            out_ref[:, width:] = folded.astype(jnp.bfloat16)

    local = pl.BlockSpec(memory_space=pltpu.VMEM)
    shapes = [pltpu.VMEM((rows, width + fold), jnp.bfloat16) for _ in shifts]
    shapes.append(pltpu.VMEM((half_count, rows * shards, 2 * rows * shards), jnp.bfloat16))
    smem = pl.BlockSpec(memory_space=pltpu.SMEM)
    return pl.pallas_call(
        body,
        in_specs=[smem, smem, pl.BlockSpec(memory_space=pl.ANY)],
        out_shape=tuple(shapes),
        out_specs=(local,) * len(shapes),
        scratch_shapes=[
            pltpu.VMEM(table_shape, jnp.bfloat16),
            pltpu.VMEM((count, samples, width), jnp.bfloat16),
            pltpu.SemaphoreType.DMA((count,)),
        ],
        name="block_sums",
    )(freq_bins, position, snapshots)


def join_matrix(position, shifts, k, half_count):
    shards = len(shifts)
    rows = SERIES * half_count
    total = shards * rows
    target = lax.broadcasted_iota(jnp.int32, (total, 1), 0)
    series = target // (shards * half_count)
    shard = target // half_count % shards
    block = target % half_count
    source = lax.broadcasted_iota(jnp.int32, (1, 2 * total), 1)
    slot, row = source // rows % shards, source % rows
    sender = jnp.zeros_like(source)
    for i, shift in enumerate(shifts):
        sender = jnp.where(slot == i, position ^ shift, sender)
    folded = source >= total
    code = jnp.where(folded, total, 0) + sender * rows + row
    own = shard * rows + block * SERIES + series
    after = (shard + 1) % shards
    early = total + after * rows + k * SERIES + series
    early = jnp.where(block == half_count - 1, early, -1)
    return jnp.where((code == own) | (code == early), 1.0, 0.0).astype(jnp.bfloat16)


def join_and_gram(received, joins, half_count, grid_total):
    shards = len(received)
    rows, span = received[0].shape
    width = span * half_count // (half_count + 1)
    fold = width // half_count
    total = shards * rows
    size = total // NF

    def body(join_ref, *refs):
        parts, (columns_ref, gram_ref) = refs[:shards], refs[shards:]
        folded = [part[:, width:] for part in parts]
        for k in range(half_count):
            own = [part[:, k * fold : (k + 1) * fold] for part in parts]
            both = jnp.concatenate(own + folded, axis=0)
            joined = jnp.dot(join_ref[k], both, preferred_element_type=jnp.float32)
            columns_ref[:, k * fold : (k + 1) * fold] = joined.astype(jnp.bfloat16)
        columns = columns_ref[...]
        products = lax.dot_general(
            columns, columns, (((1,), (1,)), ((), ())), preferred_element_type=jnp.float32
        )
        for f in range(NF):
            part = products[f * size : (f + 1) * size, f * size : (f + 1) * size]
            gram_ref[:, f * size : (f + 1) * size] = part * (1.0 / grid_total)

    return pl.pallas_call(
        body,
        in_specs=[pl.BlockSpec(memory_space=pltpu.VMEM)] * (shards + 1),
        out_shape=(
            pltpu.VMEM((total, width), jnp.bfloat16),
            pltpu.VMEM((size, NF * size), jnp.float32),
        ),
        out_specs=(pl.BlockSpec(memory_space=pltpu.VMEM),) * 2,
        name="join_and_gram",
    )(near(joins), *[near(part) for part in received])


def near(value):
    return pltpu.with_memory_space_constraint(value, pltpu.VMEM)


def spread_order(shards):
    bits = (shards - 1).bit_length()
    order = [int(f"{k:0{bits}b}"[::-1], 2) for k in range(1, shards)]
    return order + [0]


GRID = ("space", "tm")


def swapped(value, flips):
    wide, long = (lax.axis_size(name) for name in GRID)
    pairs = [
        (i * long + j, (i ^ flips[0]) * long + (j ^ flips[1]))
        for i in range(wide)
        for j in range(long)
    ]
    return lax.ppermute(value, GRID, pairs)


def exchange_rounds():
    cross = 1
    bits = [(1 << k, 0) for k in range(1, (lax.axis_size("space") - 1).bit_length())]
    bits += [(0, 1 << k) for k in range((lax.axis_size("tm") - 1).bit_length())]
    rounds = [[(cross, 0)]]
    while bits:
        (a, b), (c, d) = bits[0], bits[1] if len(bits) > 1 else (0, 0)
        flips = [(a, b), (c, d), (a + c, b + d)] if len(bits) > 1 else [(a, b)]
        rounds.append([(cross + i, j) for i, j in flips])
        bits = bits[2:]
    return rounds


def add_up(values):
    while len(values) > 1:
        values = [values[i] + values[i + 1] for i in range(0, len(values), 2)]
    return values[0]


def spread_row(block, i):
    return jnp.broadcast_to(block[i : i + 1, :], block.shape)


def block_inverse(d):
    low = [[None] * SUB for _ in range(SUB)]
    for k in range(SUB):
        scale = lax.rsqrt(d[k][k])
        for j in range(k):
            low[k][j] = low[k][j] * scale
        low[k][k] = scale
        below = [d[i][k] * scale for i in range(k + 1, SUB)]
        for i in range(k + 1, SUB):
            x = below[i - k - 1]
            for j in range(k + 1, i + 1):
                d[i][j] = d[i][j] - x * below[j - k - 1]
            for j in range(k + 1):
                term = x * low[k][j]
                low[i][j] = -term if low[i][j] is None else low[i][j] - term
    return low


def tree_sum(terms):
    while len(terms) > 1:
        pairs = [terms[i] + terms[i + 1] for i in range(0, len(terms) - 1, 2)]
        terms = pairs + terms[len(pairs) * 2 :]
    return terms[0]


def inverse_factor(gram, size):
    lanes = NF * size
    sub = lax.broadcasted_iota(jnp.int32, (SUB, lanes), 0)
    lane = lax.broadcasted_iota(jnp.int32, (SUB, lanes), 1)
    work, side = [], []
    for start in range(0, size, SUB):
        eye = jnp.where(lane % size == sub + start, 1.0, 0.0)
        work.append(gram[start : start + SUB, :] + ridge_term * eye)
        side.append(eye)
    done = []
    for step in range(size // SUB):
        start = step * SUB

        def column_of(block, m):
            first = jnp.broadcast_to(block[:, start + m : start + m + 1], (SUB, lanes))
            for f in range(1, NF):
                at = f * size + start + m
                other = jnp.broadcast_to(block[:, at : at + 1], (SUB, lanes))
                first = jnp.where(lane < f * size, first, other)
            return first

        columns = [[column_of(block, m) for m in range(SUB)] for block in work]
        head = columns[0]
        low = block_inverse(
            [[spread_row(head[j], i) for j in range(i + 1)] for i in range(SUB)]
        )

        def solve_rows(block):
            source = [spread_row(block, m) for m in range(SUB)]
            return [
                tree_sum([low[j][m] * source[m] for m in range(j + 1)]) for j in range(SUB)
            ]

        def apply_transposed(solved):
            return [
                tree_sum([low[j][m] * solved[j] for j in range(m, SUB)]) for m in range(SUB)
            ]

        solved_side = solve_rows(side[0])
        packed = solved_side[0]
        for j in range(1, SUB):
            packed = jnp.where(sub == j, solved_side[j], packed)
        done.append(packed)
        if len(work) > 1:
            top = apply_transposed(solve_rows(work[0]))
            top_side = apply_transposed(solved_side)
            work = [
                block - tree_sum([column[m] * top[m] for m in range(SUB)])
                for block, column in zip(work[1:], columns[1:])
            ]
            side = [
                block - tree_sum([column[m] * top_side[m] for m in range(SUB)])
                for block, column in zip(side[1:], columns[1:])
            ]
    return jnp.concatenate(done, axis=0)


def whiten(grams, columns):
    count = len(grams)
    size = grams[0].shape[0]
    total, width = columns.shape
    chunk = min(width, 512)
    chunks = width // chunk

    def body(*refs):
        columns_ref, gram_out, white_out, gram_ref, left_ref, white_ref, sems = refs[count:]
        total_gram = add_up([ref[...] for ref in refs[:count]])
        copies = []
        for f in range(NF):
            gram_ref[f] = total_gram[:, f * size : (f + 1) * size]
        copies.append(pltpu.make_async_copy(gram_ref, gram_out, sems.at[0]))
        copies[-1].start()
        inverse = inverse_factor(total_gram, size)
        lane = lax.broadcasted_iota(jnp.int32, (size, NF * size), 1)
        for f in range(NF):
            own = jnp.where(lane // size == f, inverse, 0.0)
            high = own.astype(jnp.bfloat16)
            rest = (own - high.astype(jnp.float32)).astype(jnp.bfloat16)
            left_ref[f * size : (f + 1) * size, : NF * size] = high
            left_ref[f * size : (f + 1) * size, NF * size :] = rest
        for k in range(chunks):
            here = pl.ds(k * chunk, chunk)
            part = columns_ref[:, here]
            both = jnp.concatenate([part, part], axis=0)
            done = jnp.dot(left_ref[...], both, preferred_element_type=jnp.float32)
            for f in range(NF):
                white_ref[f, :, here] = done[f * size : (f + 1) * size]
            copies.append(
                pltpu.make_async_copy(
                    white_ref.at[:, :, here], white_out.at[:, :, here], sems.at[k + 1]
                )
            )
            copies[-1].start()
        for copy in copies:
            copy.wait()

    return pl.pallas_call(
        body,
        in_specs=[pl.BlockSpec(memory_space=pltpu.VMEM)] * (count + 1),
        out_shape=(
            jax.ShapeDtypeStruct((NF, size, size), jnp.float32),
            jax.ShapeDtypeStruct((NF, size, width), jnp.float32),
        ),
        out_specs=(pl.BlockSpec(memory_space=pl.ANY),) * 2,
        scratch_shapes=[
            pltpu.VMEM((NF, size, size), jnp.float32),
            pltpu.VMEM((total, 2 * NF * size), jnp.bfloat16),
            pltpu.VMEM((NF, size, width), jnp.float32),
            pltpu.SemaphoreType.DMA((chunks + 1,)),
        ],
        name="whiten",
    )(*[near(gram) for gram in grams], near(columns))


def on_device(snapshots, freq_bins):
    shards = lax.axis_size("tm")
    half_count = snapshots.shape[0] // HOP
    grid_total = snapshots.shape[1] * lax.axis_size("space")
    position = lax.axis_index("tm").astype(jnp.int32)[None]
    shifts = spread_order(shards)
    *parts, joins = block_sums(freq_bins, position, snapshots, shards, shifts)
    received = []
    for shift, part in zip(shifts, parts):
        pairs = [(i, i ^ shift) for i in range(shards)]
        received.append(lax.ppermute(part, "tm", pairs) if shift else part)
    columns, gram = join_and_gram(received, joins, half_count, grid_total)
    grams = [gram]
    for flips in exchange_rounds():
        gram = add_up(grams)
        grams = [gram] + [swapped(gram, flip) for flip in flips]
    return whiten(grams, columns)


def solution(mesh):
    placed = (P("tm", "space"), P())
    return jax.shard_map(
        on_device,
        mesh=mesh,
        in_specs=placed,
        out_specs=(P(), P(None, None, ("space", "tm"))),
        check_vma=False,
    )
```

```python
import math

import jax
import jax.numpy as jnp
import numpy as np
from jax import lax
from jax.experimental import pallas as pl
from jax.experimental.pallas import tpu as pltpu
from jax.sharding import PartitionSpec as P

NFFT = 256
HOP = 128
NF = 2
SERIES = 2 * NF
SUB = 8

ridge_term = 0.01


def window_norm():
    sample = np.arange(NFFT, dtype=np.float64)
    taper = 0.5 - 0.5 * np.cos(2.0 * np.pi * sample / NFFT)
    return float(np.sqrt(np.sum(taper * taper)))


def fill_table(freq_ref, table_ref, half_count):
    row = lax.broadcasted_iota(jnp.int32, (SUB, NFFT), 0)
    sample = lax.broadcasted_iota(jnp.int32, (SUB, NFFT), 1)
    series = row % SERIES
    bins = jnp.where(series // 2 == 0, freq_ref[0], freq_ref[1])
    phase = (bins * sample + jnp.where(series % 2 == 1, NFFT // 4, 0)) % NFFT
    step = 2.0 * math.pi / NFFT
    taper = 0.5 - 0.5 * jnp.cos(step * sample.astype(jnp.float32))
    value = taper * (1.0 / window_norm()) * jnp.cos(step * phase.astype(jnp.float32))
    leading, trailing = value[:, :HOP], value[:, HOP:]
    group_of = lax.broadcasted_iota(jnp.int32, (SUB, HOP), 0) // SERIES
    per_tile = SUB // SERIES
    for first in range(0, table_ref.shape[0], 2 * SUB):
        for half in range(half_count):
            tiles = []
            for start in (first // SERIES, first // SERIES + per_tile):
                group = group_of + start
                block = jnp.where(group == half_count, -1, group)
                tile = jnp.where(half == block, leading, 0.0)
                tile = jnp.where(half == block + 1, trailing, tile)
                tiles.append(jnp.where(group > half_count, 0.0, tile))
            packed = jnp.concatenate(tiles, axis=0).astype(jnp.bfloat16)
            table_ref[first : first + 2 * SUB, half * HOP : (half + 1) * HOP] = packed


def block_sums(freq_bins, position, snapshots, shards, shifts):
    samples, points = snapshots.shape
    half_count = samples // HOP
    rows = SERIES * half_count
    width = points // shards
    fold = width // half_count
    table_shape = (rows + SUB * 2, samples)
    count = len(shifts)

    def body(freq_ref, position_ref, data_ref, *refs):
        outs, (join_ref, table_ref, buffer_ref, sems) = refs[:count], refs[count:]
        copies = []
        for i, shift in enumerate(shifts):
            first = pl.multiple_of((position_ref[0] ^ shift) * width, width)
            copies.append(
                pltpu.make_async_copy(
                    data_ref.at[:, pl.ds(first, width)], buffer_ref.at[i], sems.at[i]
                )
            )
            copies[-1].start()
        fill_table(freq_ref, table_ref, half_count)
        for k in range(half_count):
            join_ref[k] = join_matrix(position_ref[0], shifts, k, half_count)
        for copy, out_ref, i in zip(copies, outs, range(count)):
            copy.wait()
            sums = jnp.dot(table_ref[...], buffer_ref[i], preferred_element_type=jnp.float32)
            out_ref[:, :width] = sums[:rows].astype(jnp.bfloat16)
            early = sums[rows : rows + SERIES]
            folded = jnp.concatenate(
                [early[:, k * fold : (k + 1) * fold] for k in range(half_count)], axis=0
            )
            out_ref[:, width:] = folded.astype(jnp.bfloat16)

    local = pl.BlockSpec(memory_space=pltpu.VMEM)
    shapes = [pltpu.VMEM((rows, width + fold), jnp.bfloat16) for _ in shifts]
    shapes.append(pltpu.VMEM((half_count, rows * shards, 2 * rows * shards), jnp.bfloat16))
    smem = pl.BlockSpec(memory_space=pltpu.SMEM)
    return pl.pallas_call(
        body,
        in_specs=[smem, smem, pl.BlockSpec(memory_space=pl.ANY)],
        out_shape=tuple(shapes),
        out_specs=(local,) * len(shapes),
        scratch_shapes=[
            pltpu.VMEM(table_shape, jnp.bfloat16),
            pltpu.VMEM((count, samples, width), jnp.bfloat16),
            pltpu.SemaphoreType.DMA((count,)),
        ],
        name="block_sums",
    )(freq_bins, position, snapshots)


def join_matrix(position, shifts, k, half_count):
    shards = len(shifts)
    rows = SERIES * half_count
    total = shards * rows
    target = lax.broadcasted_iota(jnp.int32, (total, 1), 0)
    series = target // (shards * half_count)
    shard = target // half_count % shards
    block = target % half_count
    source = lax.broadcasted_iota(jnp.int32, (1, 2 * total), 1)
    slot, row = source // rows % shards, source % rows
    sender = jnp.zeros_like(source)
    for i, shift in enumerate(shifts):
        sender = jnp.where(slot == i, position ^ shift, sender)
    folded = source >= total
    code = jnp.where(folded, total, 0) + sender * rows + row
    own = shard * rows + block * SERIES + series
    after = (shard + 1) % shards
    early = total + after * rows + k * SERIES + series
    early = jnp.where(block == half_count - 1, early, -1)
    return jnp.where((code == own) | (code == early), 1.0, 0.0).astype(jnp.bfloat16)


def join_and_gram(received, joins, half_count, grid_total):
    shards = len(received)
    rows, span = received[0].shape
    width = span * half_count // (half_count + 1)
    fold = width // half_count
    total = shards * rows
    size = total // NF

    def body(join_ref, *refs):
        parts, (columns_ref, gram_ref) = refs[:shards], refs[shards:]
        folded = [part[:, width:] for part in parts]
        for k in range(half_count):
            own = [part[:, k * fold : (k + 1) * fold] for part in parts]
            both = jnp.concatenate(own + folded, axis=0)
            joined = jnp.dot(join_ref[k], both, preferred_element_type=jnp.float32)
            columns_ref[:, k * fold : (k + 1) * fold] = joined.astype(jnp.bfloat16)
        columns = columns_ref[...]
        products = lax.dot_general(
            columns, columns, (((1,), (1,)), ((), ())), preferred_element_type=jnp.float32
        )
        for f in range(NF):
            part = products[f * size : (f + 1) * size, f * size : (f + 1) * size]
            gram_ref[:, f * size : (f + 1) * size] = part * (1.0 / grid_total)

    return pl.pallas_call(
        body,
        in_specs=[pl.BlockSpec(memory_space=pltpu.VMEM)] * (shards + 1),
        out_shape=(
            pltpu.VMEM((total, width), jnp.bfloat16),
            pltpu.VMEM((size, NF * size), jnp.float32),
        ),
        out_specs=(pl.BlockSpec(memory_space=pltpu.VMEM),) * 2,
        name="join_and_gram",
    )(near(joins), *[near(part) for part in received])


def near(value):
    return pltpu.with_memory_space_constraint(value, pltpu.VMEM)


def reversed_bits(count):
    bits = (count - 1).bit_length()
    return [int(f"{k:0{bits}b}"[::-1], 2) for k in range(1, count)] + [0]


def spread_order(shards):
    half = shards // 2
    far = [half + k for k in reversed_bits(half)]
    order = []
    for k in range(half):
        order += [far[k], (k + 1) % half]
    return order


GRID = ("space", "tm")


def swapped(value, flips):
    wide, long = (lax.axis_size(name) for name in GRID)
    pairs = [
        (i * long + j, (i ^ flips[0]) * long + (j ^ flips[1]))
        for i in range(wide)
        for j in range(long)
    ]
    return lax.ppermute(value, GRID, pairs)


def exchange_rounds():
    cross = 1
    bits = [(1 << k, 0) for k in range(1, (lax.axis_size("space") - 1).bit_length())]
    bits += [(0, 1 << k) for k in range((lax.axis_size("tm") - 1).bit_length())]
    rounds = [[(cross, 0)]]
    while bits:
        (a, b), (c, d) = bits[0], bits[1] if len(bits) > 1 else (0, 0)
        flips = [(a, b), (c, d), (a + c, b + d)] if len(bits) > 1 else [(a, b)]
        rounds.append([(cross + i, j) for i, j in flips])
        bits = bits[2:]
    return rounds


def add_up(values):
    while len(values) > 1:
        values = [values[i] + values[i + 1] for i in range(0, len(values), 2)]
    return values[0]


def spread_row(block, i):
    return jnp.broadcast_to(block[i : i + 1, :], block.shape)


def block_inverse(d):
    low = [[None] * SUB for _ in range(SUB)]
    for k in range(SUB):
        scale = lax.rsqrt(d[k][k])
        for j in range(k):
            low[k][j] = low[k][j] * scale
        low[k][k] = scale
        below = [d[i][k] * scale for i in range(k + 1, SUB)]
        for i in range(k + 1, SUB):
            x = below[i - k - 1]
            for j in range(k + 1, i + 1):
                d[i][j] = d[i][j] - x * below[j - k - 1]
            for j in range(k + 1):
                term = x * low[k][j]
                low[i][j] = -term if low[i][j] is None else low[i][j] - term
    return low


def tree_sum(terms):
    while len(terms) > 1:
        pairs = [terms[i] + terms[i + 1] for i in range(0, len(terms) - 1, 2)]
        terms = pairs + terms[len(pairs) * 2 :]
    return terms[0]


def inverse_factor(gram, size):
    lanes = NF * size
    sub = lax.broadcasted_iota(jnp.int32, (SUB, lanes), 0)
    lane = lax.broadcasted_iota(jnp.int32, (SUB, lanes), 1)
    work, side = [], []
    for start in range(0, size, SUB):
        eye = jnp.where(lane % size == sub + start, 1.0, 0.0)
        work.append(gram[start : start + SUB, :] + ridge_term * eye)
        side.append(eye)
    done = []
    for step in range(size // SUB):
        start = step * SUB

        def column_of(block, m):
            first = jnp.broadcast_to(block[:, start + m : start + m + 1], (SUB, lanes))
            for f in range(1, NF):
                at = f * size + start + m
                other = jnp.broadcast_to(block[:, at : at + 1], (SUB, lanes))
                first = jnp.where(lane < f * size, first, other)
            return first

        columns = [[column_of(block, m) for m in range(SUB)] for block in work]
        head = columns[0]
        low = block_inverse(
            [[spread_row(head[j], i) for j in range(i + 1)] for i in range(SUB)]
        )

        def solve_rows(block):
            source = [spread_row(block, m) for m in range(SUB)]
            return [
                tree_sum([low[j][m] * source[m] for m in range(j + 1)]) for j in range(SUB)
            ]

        def apply_transposed(solved):
            return [
                tree_sum([low[j][m] * solved[j] for j in range(m, SUB)]) for m in range(SUB)
            ]

        solved_side = solve_rows(side[0])
        packed = solved_side[0]
        for j in range(1, SUB):
            packed = jnp.where(sub == j, solved_side[j], packed)
        done.append(packed)
        if len(work) > 1:
            top = apply_transposed(solve_rows(work[0]))
            top_side = apply_transposed(solved_side)
            work = [
                block - tree_sum([column[m] * top[m] for m in range(SUB)])
                for block, column in zip(work[1:], columns[1:])
            ]
            side = [
                block - tree_sum([column[m] * top_side[m] for m in range(SUB)])
                for block, column in zip(side[1:], columns[1:])
            ]
    return jnp.concatenate(done, axis=0)


def whiten(grams, columns):
    count = len(grams)
    size = grams[0].shape[0]
    total, width = columns.shape
    chunk = min(width, 512)
    chunks = width // chunk

    def body(*refs):
        columns_ref, gram_out, white_out, gram_ref, left_ref, white_ref, sems = refs[count:]
        total_gram = add_up([ref[...] for ref in refs[:count]])
        copies = []
        for f in range(NF):
            gram_ref[f] = total_gram[:, f * size : (f + 1) * size]
        copies.append(pltpu.make_async_copy(gram_ref, gram_out, sems.at[0]))
        copies[-1].start()
        inverse = inverse_factor(total_gram, size)
        lane = lax.broadcasted_iota(jnp.int32, (size, NF * size), 1)
        for f in range(NF):
            own = jnp.where(lane // size == f, inverse, 0.0)
            high = own.astype(jnp.bfloat16)
            rest = (own - high.astype(jnp.float32)).astype(jnp.bfloat16)
            left_ref[f * size : (f + 1) * size, : NF * size] = high
            left_ref[f * size : (f + 1) * size, NF * size :] = rest
        for k in range(chunks):
            here = pl.ds(k * chunk, chunk)
            part = columns_ref[:, here]
            both = jnp.concatenate([part, part], axis=0)
            done = jnp.dot(left_ref[...], both, preferred_element_type=jnp.float32)
            for f in range(NF):
                white_ref[f, :, here] = done[f * size : (f + 1) * size]
            copies.append(
                pltpu.make_async_copy(
                    white_ref.at[:, :, here], white_out.at[:, :, here], sems.at[k + 1]
                )
            )
            copies[-1].start()
        for copy in copies:
            copy.wait()

    return pl.pallas_call(
        body,
        in_specs=[pl.BlockSpec(memory_space=pltpu.VMEM)] * (count + 1),
        out_shape=(
            jax.ShapeDtypeStruct((NF, size, size), jnp.float32),
            jax.ShapeDtypeStruct((NF, size, width), jnp.float32),
        ),
        out_specs=(pl.BlockSpec(memory_space=pl.ANY),) * 2,
        scratch_shapes=[
            pltpu.VMEM((NF, size, size), jnp.float32),
            pltpu.VMEM((total, 2 * NF * size), jnp.bfloat16),
            pltpu.VMEM((NF, size, width), jnp.float32),
            pltpu.SemaphoreType.DMA((chunks + 1,)),
        ],
        name="whiten",
    )(*[near(gram) for gram in grams], near(columns))


def on_device(snapshots, freq_bins):
    shards = lax.axis_size("tm")
    half_count = snapshots.shape[0] // HOP
    grid_total = snapshots.shape[1] * lax.axis_size("space")
    position = lax.axis_index("tm").astype(jnp.int32)[None]
    shifts = spread_order(shards)
    *parts, joins = block_sums(freq_bins, position, snapshots, shards, shifts)
    received = []
    for shift, part in zip(shifts, parts):
        pairs = [(i, i ^ shift) for i in range(shards)]
        received.append(lax.ppermute(part, "tm", pairs) if shift else part)
    columns, gram = join_and_gram(received, joins, half_count, grid_total)
    grams = [gram]
    for flips in exchange_rounds():
        gram = add_up(grams)
        grams = [gram] + [swapped(gram, flip) for flip in flips]
    return whiten(grams, columns)


def solution(mesh):
    placed = (P("tm", "space"), P())
    return jax.shard_map(
        on_device,
        mesh=mesh,
        in_specs=placed,
        out_specs=(P(), P(None, None, ("space", "tm"))),
        check_vma=False,
    )
```

```python
import math

import jax
import jax.numpy as jnp
import numpy as np
from jax import lax
from jax.experimental import pallas as pl
from jax.experimental.pallas import tpu as pltpu
from jax.sharding import PartitionSpec as P

NFFT = 256
HOP = 128
NF = 2
SERIES = 2 * NF
SUB = 8

ridge_term = 0.01


def window_norm():
    sample = np.arange(NFFT, dtype=np.float64)
    taper = 0.5 - 0.5 * np.cos(2.0 * np.pi * sample / NFFT)
    return float(np.sqrt(np.sum(taper * taper)))


def fill_table(freq_ref, table_ref, half_count):
    row = lax.broadcasted_iota(jnp.int32, (SUB, NFFT), 0)
    sample = lax.broadcasted_iota(jnp.int32, (SUB, NFFT), 1)
    series = row % SERIES
    bins = jnp.where(series // 2 == 0, freq_ref[0], freq_ref[1])
    phase = (bins * sample + jnp.where(series % 2 == 1, NFFT // 4, 0)) % NFFT
    step = 2.0 * math.pi / NFFT
    taper = 0.5 - 0.5 * jnp.cos(step * sample.astype(jnp.float32))
    value = taper * (1.0 / window_norm()) * jnp.cos(step * phase.astype(jnp.float32))
    leading, trailing = value[:, :HOP], value[:, HOP:]
    group_of = lax.broadcasted_iota(jnp.int32, (SUB, HOP), 0) // SERIES
    per_tile = SUB // SERIES
    for first in range(0, table_ref.shape[0], 2 * SUB):
        for half in range(half_count):
            tiles = []
            for start in (first // SERIES, first // SERIES + per_tile):
                group = group_of + start
                block = jnp.where(group == half_count, -1, group)
                tile = jnp.where(half == block, leading, 0.0)
                tile = jnp.where(half == block + 1, trailing, tile)
                tiles.append(jnp.where(group > half_count, 0.0, tile))
            packed = jnp.concatenate(tiles, axis=0).astype(jnp.bfloat16)
            table_ref[first : first + 2 * SUB, half * HOP : (half + 1) * HOP] = packed


def block_sums(freq_bins, position, snapshots, shards, shifts):
    samples, points = snapshots.shape
    half_count = samples // HOP
    rows = SERIES * half_count
    width = points // shards
    fold = width // half_count
    table_shape = (rows + SUB * 2, samples)
    count = len(shifts)

    def body(freq_ref, position_ref, data_ref, *refs):
        outs, (join_ref, table_ref, buffer_ref, sems) = refs[:count], refs[count:]
        copies = []
        for i, shift in enumerate(shifts):
            first = pl.multiple_of((position_ref[0] ^ shift) * width, width)
            copies.append(
                pltpu.make_async_copy(
                    data_ref.at[:, pl.ds(first, width)], buffer_ref.at[i], sems.at[i]
                )
            )
            copies[-1].start()
        fill_table(freq_ref, table_ref, half_count)
        for k in range(half_count):
            join_ref[k] = join_matrix(position_ref[0], shifts, k, half_count)
        for copy, out_ref, i in zip(copies, outs, range(count)):
            copy.wait()
            sums = jnp.dot(table_ref[...], buffer_ref[i], preferred_element_type=jnp.float32)
            out_ref[:, :width] = sums[:rows].astype(jnp.bfloat16)
            early = sums[rows : rows + SERIES]
            folded = jnp.concatenate(
                [early[:, k * fold : (k + 1) * fold] for k in range(half_count)], axis=0
            )
            out_ref[:, width:] = folded.astype(jnp.bfloat16)

    local = pl.BlockSpec(memory_space=pltpu.VMEM)
    shapes = [pltpu.VMEM((rows, width + fold), jnp.bfloat16) for _ in shifts]
    shapes.append(pltpu.VMEM((half_count, rows * shards, 2 * rows * shards), jnp.bfloat16))
    smem = pl.BlockSpec(memory_space=pltpu.SMEM)
    return pl.pallas_call(
        body,
        in_specs=[smem, smem, pl.BlockSpec(memory_space=pl.ANY)],
        out_shape=tuple(shapes),
        out_specs=(local,) * len(shapes),
        scratch_shapes=[
            pltpu.VMEM(table_shape, jnp.bfloat16),
            pltpu.VMEM((count, samples, width), jnp.bfloat16),
            pltpu.SemaphoreType.DMA((count,)),
        ],
        name="block_sums",
    )(freq_bins, position, snapshots)


def join_matrix(position, shifts, k, half_count):
    shards = len(shifts)
    rows = SERIES * half_count
    total = shards * rows
    target = lax.broadcasted_iota(jnp.int32, (total, 1), 0)
    series = target // (shards * half_count)
    shard = target // half_count % shards
    block = target % half_count
    source = lax.broadcasted_iota(jnp.int32, (1, 2 * total), 1)
    slot, row = source // rows % shards, source % rows
    sender = jnp.zeros_like(source)
    for i, shift in enumerate(shifts):
        sender = jnp.where(slot == i, position ^ shift, sender)
    folded = source >= total
    code = jnp.where(folded, total, 0) + sender * rows + row
    own = shard * rows + block * SERIES + series
    after = (shard + 1) % shards
    early = total + after * rows + k * SERIES + series
    early = jnp.where(block == half_count - 1, early, -1)
    return jnp.where((code == own) | (code == early), 1.0, 0.0).astype(jnp.bfloat16)


def join_and_gram(received, joins, half_count, grid_total):
    shards = len(received)
    rows, span = received[0].shape
    width = span * half_count // (half_count + 1)
    fold = width // half_count
    total = shards * rows
    size = total // NF

    def body(join_ref, *refs):
        parts, (columns_ref, gram_ref) = refs[:shards], refs[shards:]
        folded = [part[:, width:] for part in parts]
        for k in range(half_count):
            own = [part[:, k * fold : (k + 1) * fold] for part in parts]
            both = jnp.concatenate(own + folded, axis=0)
            joined = jnp.dot(join_ref[k], both, preferred_element_type=jnp.float32)
            columns_ref[:, k * fold : (k + 1) * fold] = joined.astype(jnp.bfloat16)
        columns = columns_ref[...]
        products = lax.dot_general(
            columns, columns, (((1,), (1,)), ((), ())), preferred_element_type=jnp.float32
        )
        for f in range(NF):
            part = products[f * size : (f + 1) * size, f * size : (f + 1) * size]
            gram_ref[:, f * size : (f + 1) * size] = part * (1.0 / grid_total)

    return pl.pallas_call(
        body,
        in_specs=[pl.BlockSpec(memory_space=pltpu.VMEM)] * (shards + 1),
        out_shape=(
            pltpu.VMEM((total, width), jnp.bfloat16),
            pltpu.VMEM((size, NF * size), jnp.float32),
        ),
        out_specs=(pl.BlockSpec(memory_space=pltpu.VMEM),) * 2,
        name="join_and_gram",
    )(near(joins), *[near(part) for part in received])


def near(value):
    return pltpu.with_memory_space_constraint(value, pltpu.VMEM)


def reversed_bits(count):
    bits = (count - 1).bit_length()
    return [int(f"{k:0{bits}b}"[::-1], 2) for k in range(1, count)] + [0]


def spread_order(shards):
    half = shards // 2
    far = [half + k for k in reversed_bits(half)]
    order = []
    for k in range(half):
        order += [far[k], (k + 1) % half]
    return order


GRID = ("space", "tm")


def swapped(value, flips):
    wide, long = (lax.axis_size(name) for name in GRID)
    pairs = [
        (i * long + j, (i ^ flips[0]) * long + (j ^ flips[1]))
        for i in range(wide)
        for j in range(long)
    ]
    return lax.ppermute(value, GRID, pairs)


def exchange_rounds():
    cross = 1
    bits = [(1 << k, 0) for k in range(1, (lax.axis_size("space") - 1).bit_length())]
    bits += [(0, 1 << k) for k in range((lax.axis_size("tm") - 1).bit_length())]
    rounds = [[(cross, 0)]]
    while bits:
        (a, b), (c, d) = bits[0], bits[1] if len(bits) > 1 else (0, 0)
        flips = [(a, b), (a + c, b + d), (c, d)] if len(bits) > 1 else [(a, b)]
        rounds.append([(cross + i, j) for i, j in flips])
        bits = bits[2:]
    return rounds


def add_up(values):
    while len(values) > 1:
        values = [values[i] + values[i + 1] for i in range(0, len(values), 2)]
    return values[0]


def spread_row(block, i):
    return jnp.broadcast_to(block[i : i + 1, :], block.shape)


def block_inverse(d):
    low = [[None] * SUB for _ in range(SUB)]
    for k in range(SUB):
        scale = lax.rsqrt(d[k][k])
        for j in range(k):
            low[k][j] = low[k][j] * scale
        low[k][k] = scale
        below = [d[i][k] * scale for i in range(k + 1, SUB)]
        for i in range(k + 1, SUB):
            x = below[i - k - 1]
            for j in range(k + 1, i + 1):
                d[i][j] = d[i][j] - x * below[j - k - 1]
            for j in range(k + 1):
                term = x * low[k][j]
                low[i][j] = -term if low[i][j] is None else low[i][j] - term
    return low


def tree_sum(terms):
    while len(terms) > 1:
        pairs = [terms[i] + terms[i + 1] for i in range(0, len(terms) - 1, 2)]
        terms = pairs + terms[len(pairs) * 2 :]
    return terms[0]


def inverse_factor(gram, size):
    lanes = NF * size
    sub = lax.broadcasted_iota(jnp.int32, (SUB, lanes), 0)
    lane = lax.broadcasted_iota(jnp.int32, (SUB, lanes), 1)
    work, side = [], []
    for start in range(0, size, SUB):
        eye = jnp.where(lane % size == sub + start, 1.0, 0.0)
        work.append(gram[start : start + SUB, :] + ridge_term * eye)
        side.append(eye)
    done = []
    for step in range(size // SUB):
        start = step * SUB

        def column_of(block, m):
            first = jnp.broadcast_to(block[:, start + m : start + m + 1], (SUB, lanes))
            for f in range(1, NF):
                at = f * size + start + m
                other = jnp.broadcast_to(block[:, at : at + 1], (SUB, lanes))
                first = jnp.where(lane < f * size, first, other)
            return first

        columns = [[column_of(block, m) for m in range(SUB)] for block in work]
        head = columns[0]
        low = block_inverse(
            [[spread_row(head[j], i) for j in range(i + 1)] for i in range(SUB)]
        )

        def solve_rows(block):
            source = [spread_row(block, m) for m in range(SUB)]
            return [
                tree_sum([low[j][m] * source[m] for m in range(j + 1)]) for j in range(SUB)
            ]

        def apply_transposed(solved):
            return [
                tree_sum([low[j][m] * solved[j] for j in range(m, SUB)]) for m in range(SUB)
            ]

        solved_side = solve_rows(side[0])
        packed = solved_side[0]
        for j in range(1, SUB):
            packed = jnp.where(sub == j, solved_side[j], packed)
        done.append(packed)
        if len(work) > 1:
            top = apply_transposed(solve_rows(work[0]))
            top_side = apply_transposed(solved_side)
            work = [
                block - tree_sum([column[m] * top[m] for m in range(SUB)])
                for block, column in zip(work[1:], columns[1:])
            ]
            side = [
                block - tree_sum([column[m] * top_side[m] for m in range(SUB)])
                for block, column in zip(side[1:], columns[1:])
            ]
    return jnp.concatenate(done, axis=0)


def whiten(grams, columns):
    count = len(grams)
    size = grams[0].shape[0]
    total, width = columns.shape
    chunk = min(width, 512)
    chunks = width // chunk

    def body(*refs):
        columns_ref, gram_out, white_out, gram_ref, left_ref, white_ref, sems = refs[count:]
        total_gram = add_up([ref[...] for ref in refs[:count]])
        copies = []
        for f in range(NF):
            gram_ref[f] = total_gram[:, f * size : (f + 1) * size]
        copies.append(pltpu.make_async_copy(gram_ref, gram_out, sems.at[0]))
        copies[-1].start()
        inverse = inverse_factor(total_gram, size)
        lane = lax.broadcasted_iota(jnp.int32, (size, NF * size), 1)
        for f in range(NF):
            own = jnp.where(lane // size == f, inverse, 0.0)
            high = own.astype(jnp.bfloat16)
            rest = (own - high.astype(jnp.float32)).astype(jnp.bfloat16)
            left_ref[f * size : (f + 1) * size, : NF * size] = high
            left_ref[f * size : (f + 1) * size, NF * size :] = rest
        for k in range(chunks):
            here = pl.ds(k * chunk, chunk)
            part = columns_ref[:, here]
            both = jnp.concatenate([part, part], axis=0)
            done = jnp.dot(left_ref[...], both, preferred_element_type=jnp.float32)
            for f in range(NF):
                white_ref[f, :, here] = done[f * size : (f + 1) * size]
            copies.append(
                pltpu.make_async_copy(
                    white_ref.at[:, :, here], white_out.at[:, :, here], sems.at[k + 1]
                )
            )
            copies[-1].start()
        for copy in copies:
            copy.wait()

    return pl.pallas_call(
        body,
        in_specs=[pl.BlockSpec(memory_space=pltpu.VMEM)] * (count + 1),
        out_shape=(
            jax.ShapeDtypeStruct((NF, size, size), jnp.float32),
            jax.ShapeDtypeStruct((NF, size, width), jnp.float32),
        ),
        out_specs=(pl.BlockSpec(memory_space=pl.ANY),) * 2,
        scratch_shapes=[
            pltpu.VMEM((NF, size, size), jnp.float32),
            pltpu.VMEM((total, 2 * NF * size), jnp.bfloat16),
            pltpu.VMEM((NF, size, width), jnp.float32),
            pltpu.SemaphoreType.DMA((chunks + 1,)),
        ],
        name="whiten",
    )(*[near(gram) for gram in grams], near(columns))


def on_device(snapshots, freq_bins):
    shards = lax.axis_size("tm")
    half_count = snapshots.shape[0] // HOP
    grid_total = snapshots.shape[1] * lax.axis_size("space")
    position = lax.axis_index("tm").astype(jnp.int32)[None]
    shifts = spread_order(shards)
    *parts, joins = block_sums(freq_bins, position, snapshots, shards, shifts)
    received = []
    for shift, part in zip(shifts, parts):
        pairs = [(i, i ^ shift) for i in range(shards)]
        received.append(lax.ppermute(part, "tm", pairs) if shift else part)
    columns, gram = join_and_gram(received, joins, half_count, grid_total)
    grams = [gram]
    for flips in exchange_rounds():
        gram = add_up(grams)
        grams = [gram] + [swapped(gram, flip) for flip in flips]
    return whiten(grams, columns)


def solution(mesh):
    placed = (P("tm", "space"), P())
    return jax.shard_map(
        on_device,
        mesh=mesh,
        in_specs=placed,
        out_specs=(P(), P(None, None, ("space", "tm"))),
        check_vma=False,
    )
```

```python
import math

import jax
import jax.numpy as jnp
import numpy as np
from jax import lax
from jax.experimental import pallas as pl
from jax.experimental.pallas import tpu as pltpu
from jax.sharding import PartitionSpec as P

NFFT = 256
HOP = 128
NF = 2
SERIES = 2 * NF
SUB = 8

ridge_term = 0.01


def window_norm():
    sample = np.arange(NFFT, dtype=np.float64)
    taper = 0.5 - 0.5 * np.cos(2.0 * np.pi * sample / NFFT)
    return float(np.sqrt(np.sum(taper * taper)))


def fill_table(freq_ref, table_ref, half_count):
    row = lax.broadcasted_iota(jnp.int32, (SUB, NFFT), 0)
    sample = lax.broadcasted_iota(jnp.int32, (SUB, NFFT), 1)
    series = row % SERIES
    bins = jnp.where(series // 2 == 0, freq_ref[0], freq_ref[1])
    phase = (bins * sample + jnp.where(series % 2 == 1, NFFT // 4, 0)) % NFFT
    step = 2.0 * math.pi / NFFT
    taper = 0.5 - 0.5 * jnp.cos(step * sample.astype(jnp.float32))
    value = taper * (1.0 / window_norm()) * jnp.cos(step * phase.astype(jnp.float32))
    leading, trailing = value[:, :HOP], value[:, HOP:]
    group_of = lax.broadcasted_iota(jnp.int32, (SUB, HOP), 0) // SERIES
    per_tile = SUB // SERIES
    for first in range(0, table_ref.shape[0], 2 * SUB):
        for half in range(half_count):
            tiles = []
            for start in (first // SERIES, first // SERIES + per_tile):
                group = group_of + start
                block = jnp.where(group == half_count, -1, group)
                tile = jnp.where(half == block, leading, 0.0)
                tile = jnp.where(half == block + 1, trailing, tile)
                tiles.append(jnp.where(group > half_count, 0.0, tile))
            packed = jnp.concatenate(tiles, axis=0).astype(jnp.bfloat16)
            table_ref[first : first + 2 * SUB, half * HOP : (half + 1) * HOP] = packed


def block_sums(freq_bins, position, snapshots, shards, shifts, table=None, join_shifts=()):
    samples, points = snapshots.shape
    half_count = samples // HOP
    rows = SERIES * half_count
    width = points // shards
    fold = width // half_count
    table_shape = (rows + SUB * 2, samples)
    count = len(shifts)
    first_call = table is None

    def body(freq_ref, position_ref, data_ref, *refs):
        table_ref, outs = refs[0], refs[1:]
        buffer_ref, sems = refs[-2:]
        copies = []
        for i, shift in enumerate(shifts):
            first = pl.multiple_of((position_ref[0] ^ shift) * width, width)
            copies.append(
                pltpu.make_async_copy(
                    data_ref.at[:, pl.ds(first, width)], buffer_ref.at[i], sems.at[i]
                )
            )
            copies[-1].start()
        if first_call:
            fill_table(freq_ref, table_ref, half_count)
        if join_shifts:
            for k in range(half_count):
                outs[count][k] = join_matrix(position_ref[0], join_shifts, k, half_count)
        for copy, out_ref, i in zip(copies, outs, range(count)):
            copy.wait()
            sums = jnp.dot(table_ref[...], buffer_ref[i], preferred_element_type=jnp.float32)
            out_ref[:, :width] = sums[:rows].astype(jnp.bfloat16)
            early = sums[rows : rows + SERIES]
            folded = jnp.concatenate(
                [early[:, k * fold : (k + 1) * fold] for k in range(half_count)], axis=0
            )
            out_ref[:, width:] = folded.astype(jnp.bfloat16)

    local = pl.BlockSpec(memory_space=pltpu.VMEM)
    shapes = [pltpu.VMEM((rows, width + fold), jnp.bfloat16) for _ in shifts]
    if join_shifts:
        joins = (half_count, rows * shards, 2 * rows * shards)
        shapes.append(pltpu.VMEM(joins, jnp.bfloat16))
    operands = [freq_bins, position, snapshots]
    if first_call:
        shapes.insert(0, pltpu.VMEM(table_shape, jnp.bfloat16))
    else:
        operands.append(near(table))
    smem = pl.BlockSpec(memory_space=pltpu.SMEM)
    return pl.pallas_call(
        body,
        in_specs=[smem, smem, pl.BlockSpec(memory_space=pl.ANY)] + [local] * (len(operands) - 3),
        out_shape=tuple(shapes),
        out_specs=(local,) * len(shapes),
        scratch_shapes=[
            pltpu.VMEM((count, samples, width), jnp.bfloat16),
            pltpu.SemaphoreType.DMA((count,)),
        ],
        name="block_sums",
    )(*operands)


def join_matrix(position, shifts, k, half_count):
    shards = len(shifts)
    rows = SERIES * half_count
    total = shards * rows
    target = lax.broadcasted_iota(jnp.int32, (total, 1), 0)
    series = target // (shards * half_count)
    shard = target // half_count % shards
    block = target % half_count
    source = lax.broadcasted_iota(jnp.int32, (1, 2 * total), 1)
    slot, row = source // rows % shards, source % rows
    sender = jnp.zeros_like(source)
    for i, shift in enumerate(shifts):
        sender = jnp.where(slot == i, position ^ shift, sender)
    folded = source >= total
    code = jnp.where(folded, total, 0) + sender * rows + row
    own = shard * rows + block * SERIES + series
    after = (shard + 1) % shards
    early = total + after * rows + k * SERIES + series
    early = jnp.where(block == half_count - 1, early, -1)
    return jnp.where((code == own) | (code == early), 1.0, 0.0).astype(jnp.bfloat16)


def join_and_gram(received, joins, half_count, grid_total):
    shards = len(received)
    rows, span = received[0].shape
    width = span * half_count // (half_count + 1)
    fold = width // half_count
    total = shards * rows
    size = total // NF

    def body(join_ref, *refs):
        parts, (columns_ref, gram_ref) = refs[:shards], refs[shards:]
        folded = [part[:, width:] for part in parts]
        for k in range(half_count):
            own = [part[:, k * fold : (k + 1) * fold] for part in parts]
            both = jnp.concatenate(own + folded, axis=0)
            joined = jnp.dot(join_ref[k], both, preferred_element_type=jnp.float32)
            columns_ref[:, k * fold : (k + 1) * fold] = joined.astype(jnp.bfloat16)
        columns = columns_ref[...]
        products = lax.dot_general(
            columns, columns, (((1,), (1,)), ((), ())), preferred_element_type=jnp.float32
        )
        for f in range(NF):
            part = products[f * size : (f + 1) * size, f * size : (f + 1) * size]
            gram_ref[:, f * size : (f + 1) * size] = part * (1.0 / grid_total)

    return pl.pallas_call(
        body,
        in_specs=[pl.BlockSpec(memory_space=pltpu.VMEM)] * (shards + 1),
        out_shape=(
            pltpu.VMEM((total, width), jnp.bfloat16),
            pltpu.VMEM((size, NF * size), jnp.float32),
        ),
        out_specs=(pl.BlockSpec(memory_space=pltpu.VMEM),) * 2,
        name="join_and_gram",
    )(near(joins), *[near(part) for part in received])


def near(value):
    return pltpu.with_memory_space_constraint(value, pltpu.VMEM)


def reversed_bits(count):
    bits = (count - 1).bit_length()
    return [int(f"{k:0{bits}b}"[::-1], 2) for k in range(1, count)] + [0]


def spread_order(shards):
    half = shards // 2
    far = [half + k for k in reversed_bits(half)]
    order = []
    for k in range(half):
        order += [far[k], (k + 1) % half]
    return order


GRID = ("space", "tm")


def swapped(value, flips):
    wide, long = (lax.axis_size(name) for name in GRID)
    pairs = [
        (i * long + j, (i ^ flips[0]) * long + (j ^ flips[1]))
        for i in range(wide)
        for j in range(long)
    ]
    return lax.ppermute(value, GRID, pairs)


def exchange_rounds():
    cross = 1
    bits = [(1 << k, 0) for k in range(1, (lax.axis_size("space") - 1).bit_length())]
    bits += [(0, 1 << k) for k in range((lax.axis_size("tm") - 1).bit_length())]
    rounds = [[(cross, 0)]]
    while bits:
        (a, b), (c, d) = bits[0], bits[1] if len(bits) > 1 else (0, 0)
        flips = [(a, b), (a + c, b + d), (c, d)] if len(bits) > 1 else [(a, b)]
        rounds.append([(cross + i, j) for i, j in flips])
        bits = bits[2:]
    return rounds


def add_up(values):
    while len(values) > 1:
        values = [values[i] + values[i + 1] for i in range(0, len(values), 2)]
    return values[0]


def spread_row(block, i):
    return jnp.broadcast_to(block[i : i + 1, :], block.shape)


def block_inverse(d):
    low = [[None] * SUB for _ in range(SUB)]
    for k in range(SUB):
        scale = lax.rsqrt(d[k][k])
        for j in range(k):
            low[k][j] = low[k][j] * scale
        low[k][k] = scale
        below = [d[i][k] * scale for i in range(k + 1, SUB)]
        for i in range(k + 1, SUB):
            x = below[i - k - 1]
            for j in range(k + 1, i + 1):
                d[i][j] = d[i][j] - x * below[j - k - 1]
            for j in range(k + 1):
                term = x * low[k][j]
                low[i][j] = -term if low[i][j] is None else low[i][j] - term
    return low


def tree_sum(terms):
    while len(terms) > 1:
        pairs = [terms[i] + terms[i + 1] for i in range(0, len(terms) - 1, 2)]
        terms = pairs + terms[len(pairs) * 2 :]
    return terms[0]


def inverse_factor(gram, size):
    lanes = NF * size
    sub = lax.broadcasted_iota(jnp.int32, (SUB, lanes), 0)
    lane = lax.broadcasted_iota(jnp.int32, (SUB, lanes), 1)
    work, side = [], []
    for start in range(0, size, SUB):
        eye = jnp.where(lane % size == sub + start, 1.0, 0.0)
        work.append(gram[start : start + SUB, :] + ridge_term * eye)
        side.append(eye)
    done = []
    for step in range(size // SUB):
        start = step * SUB

        def column_of(block, m):
            first = jnp.broadcast_to(block[:, start + m : start + m + 1], (SUB, lanes))
            for f in range(1, NF):
                at = f * size + start + m
                other = jnp.broadcast_to(block[:, at : at + 1], (SUB, lanes))
                first = jnp.where(lane < f * size, first, other)
            return first

        columns = [[column_of(block, m) for m in range(SUB)] for block in work]
        head = columns[0]
        low = block_inverse(
            [[spread_row(head[j], i) for j in range(i + 1)] for i in range(SUB)]
        )

        def solve_rows(block):
            source = [spread_row(block, m) for m in range(SUB)]
            return [
                tree_sum([low[j][m] * source[m] for m in range(j + 1)]) for j in range(SUB)
            ]

        def apply_transposed(solved):
            return [
                tree_sum([low[j][m] * solved[j] for j in range(m, SUB)]) for m in range(SUB)
            ]

        solved_side = solve_rows(side[0])
        packed = solved_side[0]
        for j in range(1, SUB):
            packed = jnp.where(sub == j, solved_side[j], packed)
        done.append(packed)
        if len(work) > 1:
            top = apply_transposed(solve_rows(work[0]))
            top_side = apply_transposed(solved_side)
            work = [
                block - tree_sum([column[m] * top[m] for m in range(SUB)])
                for block, column in zip(work[1:], columns[1:])
            ]
            side = [
                block - tree_sum([column[m] * top_side[m] for m in range(SUB)])
                for block, column in zip(side[1:], columns[1:])
            ]
    return jnp.concatenate(done, axis=0)


def whiten(grams, columns):
    count = len(grams)
    size = grams[0].shape[0]
    total, width = columns.shape
    chunk = min(width, 512)
    chunks = width // chunk

    def body(*refs):
        columns_ref, gram_out, white_out, gram_ref, left_ref, white_ref, sems = refs[count:]
        total_gram = add_up([ref[...] for ref in refs[:count]])
        copies = []
        for f in range(NF):
            gram_ref[f] = total_gram[:, f * size : (f + 1) * size]
        copies.append(pltpu.make_async_copy(gram_ref, gram_out, sems.at[0]))
        copies[-1].start()
        inverse = inverse_factor(total_gram, size)
        lane = lax.broadcasted_iota(jnp.int32, (size, NF * size), 1)
        for f in range(NF):
            own = jnp.where(lane // size == f, inverse, 0.0)
            high = own.astype(jnp.bfloat16)
            rest = (own - high.astype(jnp.float32)).astype(jnp.bfloat16)
            left_ref[f * size : (f + 1) * size, : NF * size] = high
            left_ref[f * size : (f + 1) * size, NF * size :] = rest
        for k in range(chunks):
            here = pl.ds(k * chunk, chunk)
            part = columns_ref[:, here]
            both = jnp.concatenate([part, part], axis=0)
            done = jnp.dot(left_ref[...], both, preferred_element_type=jnp.float32)
            for f in range(NF):
                white_ref[f, :, here] = done[f * size : (f + 1) * size]
            copies.append(
                pltpu.make_async_copy(
                    white_ref.at[:, :, here], white_out.at[:, :, here], sems.at[k + 1]
                )
            )
            copies[-1].start()
        for copy in copies:
            copy.wait()

    return pl.pallas_call(
        body,
        in_specs=[pl.BlockSpec(memory_space=pltpu.VMEM)] * (count + 1),
        out_shape=(
            jax.ShapeDtypeStruct((NF, size, size), jnp.float32),
            jax.ShapeDtypeStruct((NF, size, width), jnp.float32),
        ),
        out_specs=(pl.BlockSpec(memory_space=pl.ANY),) * 2,
        scratch_shapes=[
            pltpu.VMEM((NF, size, size), jnp.float32),
            pltpu.VMEM((total, 2 * NF * size), jnp.bfloat16),
            pltpu.VMEM((NF, size, width), jnp.float32),
            pltpu.SemaphoreType.DMA((chunks + 1,)),
        ],
        name="whiten",
    )(*[near(gram) for gram in grams], near(columns))


def on_device(snapshots, freq_bins):
    shards = lax.axis_size("tm")
    half_count = snapshots.shape[0] // HOP
    grid_total = snapshots.shape[1] * lax.axis_size("space")
    position = lax.axis_index("tm").astype(jnp.int32)[None]
    order = spread_order(shards)
    groups = [order[:-1], order[-1:]]
    shifts = [shift for group in groups for shift in group]
    received, table, joins = [], None, None
    for group in groups:
        done = shifts if group is groups[-1] else ()
        parts = list(block_sums(freq_bins, position, snapshots, shards, group, table, done))
        if table is None:
            table = parts.pop(0)
        if done:
            joins = parts.pop()
        for shift, part in zip(group, parts):
            pairs = [(i, i ^ shift) for i in range(shards)]
            received.append(lax.ppermute(part, "tm", pairs) if shift else part)
    columns, gram = join_and_gram(received, joins, half_count, grid_total)
    grams = [gram]
    for flips in exchange_rounds():
        gram = add_up(grams)
        grams = [gram] + [swapped(gram, flip) for flip in flips]
    return whiten(grams, columns)


def solution(mesh):
    placed = (P("tm", "space"), P())
    return jax.shard_map(
        on_device,
        mesh=mesh,
        in_specs=placed,
        out_specs=(P(), P(None, None, ("space", "tm"))),
        check_vma=False,
    )
```
